512 devices in a mesh: lat: 32 (over x, z), lon: 16 (over y, core).
Axes of the slice: x: 4, y: 8, z: 8, core: 2. Of those that a mesh axis runs over, the one named last changes fastest.
Arguments:
- tangent: float32 [256, 3, 128, 2048], P(None, None, 'lat', 'lon'), may hold values from -40 to 40
- base_state: float32 [4, 128, 2048], P(None, 'lat', 'lon'), may hold values from -0.4 to 0.8
Outputs:
- fields: float32 [256, 3, 128, 2048], P(None, None, 'lat', 'lon')
- upper: float32 [256, 256], replicated
The draws below stay inside these ranges and needn't reach their ends.
All inputs are finite; a program needn't handle non-finite values.
Results may differ from the reference program's by a relative error of at most 0.00012.
Values sent between devices are 32-bit elements; how exact they have to be, the bound alone decides.
No kernel may reach another device: no remote copies, remote signals or barrier semaphores. Data moves between devices by JAX's collectives and lax.ppermute only.
A program may use at most 64 MiB of HBM per device.

```python
import math
import jax
import jax.numpy as jnp
from jax import lax

VECS = 256
FIELDS = 3
NLAT = 128
NLON = 2048


def draw_tangent(key, part):
    first_key, second_key, third_key = jax.random.split(jax.random.fold_in(key, 11), 3)
    gaussian = jax.random.normal(first_key, (VECS, FIELDS, NLAT, NLON), jnp.float32)
    vector_scale = jnp.exp(jax.random.uniform(second_key, (VECS, 1, 1, 1), jnp.float32, 0.0, math.log(8.0)))
    cell_scale = jnp.exp(jax.random.uniform(third_key, (1, 1, NLAT, NLON), jnp.float32, math.log(0.5), math.log(2.0)))
    values = gaussian * vector_scale * cell_scale
    return jnp.clip(values, -40.0, 40.0)


def draw_base_state(key, part):
    first_key, second_key, third_key = jax.random.split(jax.random.fold_in(key, 23), 3)
    drifts = jax.random.uniform(first_key, (2, NLAT, NLON), jnp.float32, -0.4, 0.4)
    depth_field = jnp.exp(jax.random.uniform(second_key, (1, NLAT, NLON), jnp.float32, math.log(0.2), math.log(0.8)))
    rotation = jax.random.uniform(third_key, (1, NLAT, NLON), jnp.float32, 0.1, 0.5)
    return jnp.concatenate([drifts, depth_field, rotation], axis=0)


def setup_inputs(seed: int = 0) -> dict:
    key_of = jax.random.split(jax.random.key(seed), 3)
    tangent = draw_tangent(jax.random.fold_in(key_of[2], 71), 0)
    base_state = draw_base_state(jax.random.fold_in(key_of[2], 71), 0)
    return dict(tangent=tangent, base_state=base_state)


gravity_coef = 0.5

def east_west(field):
    return 0.5 * (field[..., 1:-1, 2:] - field[..., 1:-1, :-2])

def north_south(field):
    return 0.5 * (field[..., 2:, 1:-1] - field[..., :-2, 1:-1])

def advance(padded, coefficients):
    thickness = padded[:, 0]
    zonal = padded[:, 1]
    meridional = padded[:, 2]
    centre = padded[:, :, 1:-1, 1:-1]
    drift_x = coefficients[0]
    drift_y = coefficients[1]
    depth_field = coefficients[2]
    rotation = coefficients[3]

    def carried(field):
        return drift_x * east_west(field) + drift_y * north_south(field)
    new_thick = centre[:, 0] - carried(thickness) - depth_field * (east_west(zonal) + north_south(meridional))
    new_zonal = centre[:, 1] - carried(zonal) + rotation * centre[:, 2] - gravity_coef * east_west(thickness)
    new_merid = centre[:, 2] - carried(meridional) - rotation * centre[:, 1] - gravity_coef * north_south(thickness)
    return jnp.stack([new_thick, new_zonal, new_merid], axis=1)

def pad_global(state):
    wrapped = jnp.concatenate([state[..., -1:], state, state[..., :1]], axis=-1)
    return jnp.pad(wrapped, ((0, 0), (0, 0), (1, 1), (0, 0)))

def reference(tangent, base_state):
    blocks = tangent.reshape(VECS // 16, 16, FIELDS, NLAT, NLON)

    def evolve(block):
        first = advance(pad_global(block), base_state)
        return advance(pad_global(first), base_state)
    stepped = lax.map(evolve, blocks).reshape(VECS, FIELDS * NLAT * NLON)
    gram = jnp.dot(stepped.astype(jnp.float32), stepped.T.astype(jnp.float32), precision=lax.Precision.HIGHEST, preferred_element_type=jnp.float32) / (NLAT * NLON)
    lower_factor = jnp.linalg.cholesky(gram)
    fields = lax.linalg.triangular_solve(lower_factor, stepped, left_side=True, lower=True)
    return (fields.reshape(VECS, FIELDS, NLAT, NLON), lower_factor.T)
```

```python
import jax
import jax.numpy as jnp
from jax import lax
from jax.experimental import pallas as pl
from jax.experimental.pallas import tpu as pltpu
from jax.sharding import PartitionSpec as P

HI = lax.Precision.HIGHEST
F32 = jnp.float32


def iota(shape, dim):
    return lax.broadcasted_iota(jnp.int32, shape, dim)


def rows_out(x_ref, base_ref, up_ref, down_ref):
    for f in range(3):
        for k in range(2):
            place = pl.ds((2 * f + k) * 256, 256)
            up_ref[place, :] = x_ref[pl.ds(4 * f + 2 + k, 256, stride=12), :]
            down_ref[place, :] = x_ref[pl.ds(4 * f + k, 256, stride=12), :]
    blank = jnp.zeros((4, 128), F32)
    up_ref[1536:1544, :] = jnp.concatenate([base_ref[pl.ds(3, 4, stride=4), :], blank], axis=0)
    down_ref[1536:1544, :] = jnp.concatenate([base_ref[pl.ds(0, 4, stride=4), :], blank], axis=0)


def columns_out(x_ref, base_ref, pack_ref):
    lane = iota((8, 128), 1)

    def gather(read, fields):
        acc = jnp.zeros((8, 128), F32)
        for f in range(fields):
            for r in range(4):
                at = 32 * f + 8 * r
                moved = pltpu.roll(read(f, r), (at + 2) % 128, 1)
                acc = jnp.where((lane >= at) & (lane < at + 4), moved, acc)
        return acc + pltpu.roll(acc, 4, 1)

    def chunk(i, carry):
        def read(f, r):
            return x_ref[pl.ds(96 * i + 4 * f + r, 8, stride=12), :]

        pack_ref[pl.ds(pl.multiple_of(8 * i, 8), 8), :] = gather(read, 3)
        return carry

    lax.fori_loop(0, 32, chunk, 0)

    def read_base(f, r):
        rows = base_ref[pl.ds(r, 4, stride=4), :]
        return jnp.concatenate([rows, rows], axis=0)

    pack_ref[256:264, :] = gather(read_base, 1)


def corners_out(west_ref, east_ref, up_ref, down_ref):
    slot = iota((256, 128), 1) % 8
    joined = jnp.where(slot < 4, west_ref[0:256, :], east_ref[0:256, :])
    row = iota((8, 128), 0)
    lane = iota((8, 128), 1)
    for ref, r in ((up_ref, 3), (down_ref, 0)):
        at = 32 * (row // 2) + 8 * r + jnp.where(row % 2 == 0, 1, 6)
        pick = jnp.where((lane == at) & (row < 6), 1.0, 0.0)
        ref[...] = lax.dot_general(
            pick, joined, (((1,), (1,)), ((), ())), precision=HI, preferred_element_type=F32
        )


def spread_corners(corner, r):
    row = iota((8, 128), 0)
    lane = iota((8, 128), 1)
    at = 32 * (row // 2) + 8 * r
    west = (row % 2 == 0) & (lane == at + 1)
    east = (row % 2 == 1) & ((lane == at) | (lane == at + 6))
    place = jnp.where((west | east) & (row < 6), 1.0, 0.0)
    return lax.dot_general(
        corner, place, (((0,), (0,)), ((), ())), precision=HI, preferred_element_type=F32
    )


def steps(
    inside_ref, x_ref, base_ref, south_ref, north_ref, pack_ref, west_ref, east_ref,
    south_corner_ref, north_corner_ref, s_ref, gram_ref, coef_ref, cs_ref, cn_ref,
):
    lane = iota((8, 128), 1)
    slot = lane % 8
    has_south = inside_ref[0].astype(F32)
    has_north = inside_ref[1].astype(F32)
    cs_ref[...] = spread_corners(south_corner_ref[...], 0)
    cn_ref[...] = spread_corners(north_corner_ref[...], 3)

    for plane in range(4):
        scale = 1.0 if plane == 3 else 0.5
        for r in range(-1, 5):
            if r == -1:
                line = south_ref[1536 + plane:1537 + plane, :]
            elif r == 4:
                line = north_ref[1536 + plane:1537 + plane, :]
            else:
                line = base_ref[4 * plane + r:4 * plane + r + 1, :]
            coef_ref[4 * (r + 1) + plane] = jnp.broadcast_to(scale * line, (8, 128))
        row = slice(256 + plane, 257 + plane)
        line = jnp.where(slot[0:1] < 2, west_ref[row, :], jnp.where(slot[0:1] >= 6, east_ref[row, :], pack_ref[row, :]))
        coef_ref[24 + plane] = jnp.broadcast_to(scale * line, (8, 128))

    def update(q, dx, dy, at):
        a, b, c, d = (coef_ref[4 * at + k] for k in range(4))
        h = q[0] - a * dx[0] - b * dy[0] - c * (dx[1] + dy[2])
        u = q[1] - a * dx[1] - b * dy[1] + d * q[2] - 0.25 * dx[0]
        v = q[2] - a * dx[2] - b * dy[2] - d * q[1] - 0.25 * dy[0]
        return [h, u, v]

    def across(x, ends, r):
        ends = pltpu.roll(ends, (127 - 8 * r) % 128, 1)
        east = jnp.where(lane == 127, ends, pltpu.roll(x, 127, 1))
        west = jnp.where(lane == 0, ends, pltpu.roll(x, 1, 1))
        return east - west

    def beside(edge):
        return jnp.where(slot == 0, pltpu.roll(edge, 122, 1), edge)

    def chunk(i, carry):
        at = pl.ds(pl.multiple_of(8 * i, 8), 8)
        q = {}
        for f in range(3):
            for k in range(2):
                halo = pl.ds(pl.multiple_of((2 * f + k) * 256 + 8 * i, 8), 8)
                q[f, k - 2] = south_ref[halo, :]
                q[f, k + 4] = north_ref[halo, :]
            for r in range(4):
                q[f, r] = x_ref[pl.ds(96 * i + 4 * f + r, 8, stride=12), :]
        joined = jnp.where(slot < 2, west_ref[at, :], jnp.where(slot >= 6, east_ref[at, :], pack_ref[at, :]))
        cs = cs_ref[at, :]
        cn = cn_ref[at, :]

        def by_field(x):
            return [x, pltpu.roll(x, 96, 1), pltpu.roll(x, 64, 1)]

        edge, cs, cn = by_field(joined), by_field(cs), by_field(cn)
        ends = [beside(e) for e in edge]
        one = {}
        for r in range(-1, 5):
            where = cs if r == -1 else cn if r == 4 else ends
            place = 0 if r == -1 else 3 if r == 4 else r
            dx = [across(q[f, r], where[f], place) for f in range(3)]
            dy = [q[f, r + 1] - q[f, r - 1] for f in range(3)]
            new = update([q[f, r] for f in range(3)], dx, dy, r + 1)
            for f in range(3):
                one[f, r] = new[f] * has_south if r == -1 else new[f] * has_north if r == 4 else new[f]
        dx = [pltpu.roll(e, 127, 1) - pltpu.roll(e, 1, 1) for e in edge]
        dy = [
            jnp.where(lane < 24, pltpu.roll(edge[f], 120, 1), cn[f])
            - jnp.where(lane >= 8, pltpu.roll(edge[f], 8, 1), cs[f])
            for f in range(3)
        ]
        ends = [beside(e) for e in update(edge, dx, dy, 6)]
        for r in range(4):
            dx = [across(one[f, r], ends[f], r) for f in range(3)]
            dy = [one[f, r + 1] - one[f, r - 1] for f in range(3)]
            new = update([one[f, r] for f in range(3)], dx, dy, r + 1)
            for f in range(3):
                s_ref[4 * f + r, at, :] = new[f]
        return carry

    lax.fori_loop(0, 32, chunk, 0)
    total = jnp.zeros((256, 256), F32)
    for c in range(0, 12, 2):
        both = jnp.concatenate([s_ref[c], s_ref[c + 1]], axis=1)
        total = total + lax.dot_general(
            both, both, (((1,), (1,)), ((), ())), precision=HI, preferred_element_type=F32
        )
    for k, block in enumerate((total[:128, :128], total[128:, :128], total[128:, 128:])):
        for part in range(16):
            lo, hi = max(24 * part, 128 * k), min(24 * part + 24, 128 * k + 128)
            if lo < hi:
                gram_ref[part, lo - 24 * part:hi - 24 * part, :] = block[lo - 128 * k:hi - 128 * k, :]


def sum_copies(in_ref, out_ref):
    total = in_ref[0]
    for k in range(1, in_ref.shape[0]):
        total = total + in_ref[k]
    for k in range(out_ref.shape[0]):
        out_ref[k] = total


def lanes_of(x, lane):
    return jnp.broadcast_to(x[:, lane:lane + 1], x.shape)


def row_of(x, row):
    return jnp.broadcast_to(x[row:row + 1, :], x.shape)


def refined_rsqrt(d):
    r = lax.rsqrt(d)
    return r * (1.5 - 0.5 * d * r * r)


def factor_block(columns):
    e = {(i, m): row_of(columns[m], i) for m in range(8) for i in range(m, 8)}
    w = {}
    low = {}
    for k in range(8):
        r = refined_rsqrt(e[k, k])
        for i in range(k + 1, 8):
            low[i, k] = e[i, k] * r
        for m in range(k + 1, 8):
            for i in range(m, 8):
                e[i, m] = e[i, m] - low[i, k] * low[m, k]
        w[k, k] = r
        for j in range(k):
            acc = low[k, j] * w[j, j]
            for m in range(j + 1, k):
                acc = acc + low[k, m] * w[m, j]
            w[k, j] = -(acc * r)
    return w


def eliminate(m_ref):
    sub = iota((8, 128), 0)
    for panel in range(8):
        j0 = 32 * panel
        td = j0 // 128
        tiles = (0, 1, 2) if td == 0 else (1, 2, 3)
        rows = [{t: m_ref[j0 + 8 * g:j0 + 8 * g + 8, 128 * t:128 * t + 128] for t in tiles} for g in range(4)]
        for b in range(4):
            lane = j0 % 128 + 8 * b
            pivot = rows[b]
            w = factor_block([lanes_of(pivot[td], lane + m) for m in range(8)])
            wcol = []
            for k in range(8):
                c = w[7, k]
                for i in range(6, k - 1, -1):
                    c = jnp.where(sub <= i, w[i, k], c)
                if k:
                    c = jnp.where(sub < k, 0.0, c)
                wcol.append(c)
            done = {}
            for t in tiles:
                acc = wcol[0] * row_of(pivot[t], 0)
                for k in range(1, 8):
                    acc = acc + wcol[k] * row_of(pivot[t], k)
                done[t] = acc
                m_ref[j0 + 8 * b:j0 + 8 * b + 8, 128 * t:128 * t + 128] = acc
            rows[b] = done
            spread = {t: [row_of(done[t], k) for k in range(8)] for t in tiles}
            for g in range(b + 1, 4):
                left = [lanes_of(rows[g][td], lane + m) for m in range(8)]
                coef = []
                for k in range(8):
                    c = w[k, 0] * left[0]
                    for m in range(1, k + 1):
                        c = c + w[k, m] * left[m]
                    coef.append(c)
                for t in tiles:
                    x = rows[g][t]
                    s0 = coef[0] * spread[t][0]
                    s1 = coef[1] * spread[t][1]
                    for k in range(2, 8, 2):
                        s0 = s0 + coef[k] * spread[t][k]
                        s1 = s1 + coef[k + 1] * spread[t][k + 1]
                    rows[g][t] = x - (s0 + s1)
        if panel == 7:
            break
        first = j0 + 32
        top = jnp.concatenate([jnp.concatenate([rows[g][t] for t in tiles], axis=1) for g in range(4)], axis=0)
        for half in range(first // 128, 2):
            col = 128 * (half - td)
            begin = max(first, 128 * half)
            use = top if half == td else top[:, 128:]
            delta = lax.dot_general(top[:, col:col + 128], use, (((0,), (0,)), ((), ())),
                                    precision=HI, preferred_element_type=jnp.float32)
            lo = 128 * tiles[0] if half == td else 128 * tiles[1]
            hi = 128 * (tiles[-1] + 1)
            m_ref[begin:128 * half + 128, lo:hi] = m_ref[begin:128 * half + 128, lo:hi] - delta[begin - 128 * half:, :]


def chol_fields(gram_ref, s_ref, out_ref, upper_ref, m_ref, *, cells):
    row = iota((128, 128), 0)
    col = iota((128, 128), 1)
    eye = jnp.where(row == col, 1.0, 0.0).astype(F32)
    blank = jnp.zeros((128, 128), F32)
    scaled = gram_ref[...] * (1.0 / cells)
    m_ref[0:128, 0:128] = scaled[0:128]
    m_ref[128:256, 0:128] = scaled[128:256]
    m_ref[0:128, 128:256] = scaled[128:256].T
    m_ref[128:256, 128:256] = scaled[256:384]
    m_ref[0:128, 256:384] = eye
    m_ref[0:128, 384:512] = blank
    m_ref[128:256, 256:384] = blank
    m_ref[128:256, 384:512] = eye
    eliminate(m_ref)
    upper_ref[0:128, 0:128] = jnp.where(row <= col, m_ref[0:128, 0:128], 0.0)
    upper_ref[0:128, 128:256] = m_ref[0:128, 128:256]
    upper_ref[128:256, 0:128] = blank
    upper_ref[128:256, 128:256] = jnp.where(row <= col, m_ref[128:256, 128:256], 0.0)
    first = jnp.where(row >= col, m_ref[0:128, 256:384], 0.0)
    second = jnp.concatenate([m_ref[128:256, 256:384], jnp.where(row >= col, m_ref[128:256, 384:512], 0.0)], axis=1)
    inverse = jnp.concatenate([jnp.concatenate([first, blank], axis=1), second], axis=0)
    for c in range(0, 12, 2):
        both = jnp.concatenate([s_ref[c], s_ref[c + 1]], axis=1)
        y = jnp.dot(inverse, both, precision=HI, preferred_element_type=F32)
        out_ref[pl.ds(c, 256, stride=12), :] = y[:, :128]
        out_ref[pl.ds(c + 1, 256, stride=12), :] = y[:, 128:]


def shaped(*shapes):
    return tuple(jax.ShapeDtypeStruct(s, F32) for s in shapes)


def per_device(tangent, base_state):
    n_lat = lax.axis_size("lat")
    n_lon = lax.axis_size("lon")
    x = tangent.reshape(3072, 128)
    base = base_state.reshape(16, 128)
    up_rows, down_rows = pl.pallas_call(rows_out, out_shape=shaped((1544, 128), (1544, 128)))(x, base)
    pack = pl.pallas_call(columns_out, out_shape=shaped((264, 128))[0])(x, base)
    east_ring = [(i, (i + 1) % n_lon) for i in range(n_lon)]
    west_ring = [(j, i) for i, j in east_ring]
    north_line = [(i, i + 1) for i in range(n_lat - 1)]
    south_line = [(j, i) for i, j in north_line]
    south = lax.ppermute(up_rows, "lat", north_line)
    north = lax.ppermute(down_rows, "lat", south_line)
    west = lax.ppermute(pack, "lon", east_ring)
    east = lax.ppermute(pack, "lon", west_ring)
    corner_up, corner_down = pl.pallas_call(corners_out, out_shape=shaped((8, 256), (8, 256)))(west, east)
    south_corner = lax.ppermute(corner_up, "lat", north_line)
    north_corner = lax.ppermute(corner_down, "lat", south_line)
    index = lax.axis_index("lat")
    inside = jnp.stack([index > 0, index < n_lat - 1]).astype(jnp.int32)
    vmem = pl.BlockSpec(memory_space=pltpu.VMEM)
    stepped, gram = pl.pallas_call(
        steps,
        out_shape=shaped((12, 256, 128), (16, 24, 128)),
        in_specs=[pl.BlockSpec(memory_space=pltpu.SMEM)] + [vmem] * 9,
        scratch_shapes=[pltpu.VMEM((28, 8, 128), F32), pltpu.VMEM((256, 128), F32), pltpu.VMEM((256, 128), F32)],
    )(inside, x, base, south, north, pack, west, east, south_corner, north_corner)
    gram = lax.all_to_all(gram, "lon", 0, 0, tiled=True)
    gram = pl.pallas_call(sum_copies, out_shape=shaped((n_lat, 24, 128))[0])(gram)
    gram = lax.all_to_all(gram, "lat", 0, 0, tiled=True)
    gram = pl.pallas_call(sum_copies, out_shape=shaped((n_lon, 24, 128))[0])(gram)
    gram = lax.all_to_all(gram, "lon", 0, 0, tiled=True)
    cells = 4 * 128 * n_lat * n_lon
    fields, upper = pl.pallas_call(
        lambda *refs: chol_fields(*refs, cells=cells),
        out_shape=shaped((3072, 128), (256, 256)),
        scratch_shapes=[pltpu.VMEM((256, 512), F32)],
    )(gram.reshape(384, 128), stepped)
    return (fields.reshape(tangent.shape), upper)


def solution(mesh):
    in_specs = (P(None, None, "lat", "lon"), P(None, "lat", "lon"))
    out_specs = (P(None, None, "lat", "lon"), P())
    return jax.shard_map(
        per_device, mesh=mesh, in_specs=in_specs, out_specs=out_specs, check_vma=False
    )
```

```python
import jax
import jax.numpy as jnp
from jax import lax
from jax.experimental import pallas as pl
from jax.experimental.pallas import tpu as pltpu
from jax.sharding import PartitionSpec as P

HI = lax.Precision.HIGHEST
F32 = jnp.float32


def iota(shape, dim):
    return lax.broadcasted_iota(jnp.int32, shape, dim)


def eight(i):
    return pl.ds(pl.multiple_of(8 * i, 8), 8)


def split_rows(x_ref, base_ref, low_ref, high_ref, pack_ref):
    lane = iota((8, 128), 1)
    slot = lane % 32
    field = lane // 32

    def packed(parts):
        acc = jnp.zeros((8, 128), F32)
        for f, r, part in parts:
            at = 32 * f + 8 * r
            moved = pltpu.roll(part, (at + 2) % 128, 1)
            acc = acc + jnp.where((field == f) & (slot >= 8 * r) & (slot < 8 * r + 4), moved, 0.0)
        return acc + pltpu.roll(acc, 4, 1)

    def chunk(i, carry):
        for half in range(2):
            parts = []
            for f in range(3):
                for r in range(4):
                    part = x_ref[pl.ds(192 * i + 96 * half + 4 * f + r, 8, stride=12), :]
                    ref = low_ref if r < 2 else high_ref
                    start = ((r % 2) * 3 + f) * 256
                    ref[pl.ds(pl.multiple_of(start + 16 * i + 8 * half, 8), 8), :] = part
                    parts.append((f, r, part))
            pack_ref[eight(2 * i + half), :] = packed(parts)
        return carry

    lax.fori_loop(0, 16, chunk, 0)
    parts = []
    for r in range(4):
        rows = base_ref[pl.ds(r, 4, stride=4), :]
        both = jnp.concatenate([rows, rows], axis=0)
        parts.append((0, r, both))
        if r == 0:
            low_ref[1536:1544, :] = both
        if r == 3:
            high_ref[1536:1544, :] = both
    pack_ref[256:264, :] = packed(parts)


def corners_out(west_ref, east_ref, up_ref, down_ref):
    slot = iota((256, 128), 1) % 8
    joined = jnp.where(slot < 4, west_ref[0:256, :], east_ref[0:256, :])
    row = iota((8, 128), 0)
    lane = iota((8, 128), 1)
    for ref, r in ((up_ref, 3), (down_ref, 0)):
        at = 32 * (row // 2) + 8 * r + jnp.where(row % 2 == 0, 1, 6)
        pick = jnp.where((lane == at) & (row < 6), 1.0, 0.0)
        ref[...] = lax.dot_general(
            pick, joined, (((1,), (1,)), ((), ())), precision=HI, preferred_element_type=F32
        )


def spread_corners(corner, r):
    row = iota((8, 128), 0)
    lane = iota((8, 128), 1)
    at = 32 * (row // 2) + 8 * r
    west = (row % 2 == 0) & (lane == at + 1)
    east = (row % 2 == 1) & ((lane == at) | (lane == at + 6))
    place = jnp.where((west | east) & (row < 6), 1.0, 0.0)
    return lax.dot_general(
        corner, place, (((0,), (0,)), ((), ())), precision=HI, preferred_element_type=F32
    )


def set_coefs(coef_ref, at, lines):
    for plane, line in enumerate(lines):
        coef_ref[4 * at + plane] = jnp.broadcast_to((1.0 if plane == 3 else 0.5) * line, (8, 128))


def edge_lines(pack_ref, west_ref, east_ref):
    slot = iota((1, 128), 1) % 8
    for plane in range(4):
        row = slice(256 + plane, 257 + plane)
        yield jnp.where(slot < 2, west_ref[row, :], jnp.where(slot >= 6, east_ref[row, :], pack_ref[row, :]))


def advanced(coef_ref, at, q, dx, dy):
    a, b, c, d = (coef_ref[4 * at + k] for k in range(4))
    h = q[0] - a * dx[0] - b * dy[0] - c * (dx[1] + dy[2])
    u = q[1] - a * dx[1] - b * dy[1] + d * q[2] - 0.25 * dx[0]
    v = q[2] - a * dx[2] - b * dy[2] - d * q[1] - 0.25 * dy[0]
    return [h, u, v]


def from_north(coef_ref, at, q):
    b, c = (coef_ref[4 * at + k] for k in (1, 2))
    return [-(b * q[0]) - c * q[2], -(b * q[1]), -(b * q[2]) - 0.25 * q[0]]


def minus(q):
    return [-x for x in q]


def plus(p, q):
    return [x + y for x, y in zip(p, q)]


def across(lane, x, ends, r):
    ends = pltpu.roll(ends, (127 - 8 * r) % 128, 1)
    east = jnp.where(lane == 127, ends, pltpu.roll(x, 127, 1))
    west = jnp.where(lane == 0, ends, pltpu.roll(x, 1, 1))
    return east - west


def beside(lane, edge):
    return jnp.where(lane % 8 == 0, pltpu.roll(edge, 122, 1), edge)


def by_field(x):
    return [x, pltpu.roll(x, 96, 1), pltpu.roll(x, 64, 1)]


def read_row(ref, r, i):
    return [ref[pl.ds(pl.multiple_of((3 * r + f) * 256 + 8 * i, 8), 8), :] for f in range(3)]


def own_part(base_ref, low_ref, high_ref, pack_ref, west_ref, east_ref, s_low_ref, s_high_ref, coef_ref):
    lane = iota((8, 128), 1)
    slot = lane % 8
    for r in range(4):
        set_coefs(coef_ref, r, [base_ref[4 * k + r:4 * k + r + 1, :] for k in range(4)])
    set_coefs(coef_ref, 4, edge_lines(pack_ref, west_ref, east_ref))

    def step(q, edge):
        ends = [beside(lane, e) for e in edge]
        out = []
        for r in range(4):
            dx = [across(lane, q[r][f], ends[f], r) for f in range(3)]
            if r == 0:
                dy = q[1]
            elif r == 3:
                dy = minus(q[2])
            else:
                dy = plus(q[r + 1], minus(q[r - 1]))
            out.append(advanced(coef_ref, r, q[r], dx, dy))
        return out

    def chunk(i, carry):
        q = [read_row(low_ref if r < 2 else high_ref, r % 2, i) for r in range(4)]
        at = eight(i)
        joined = jnp.where(slot < 2, west_ref[at, :], jnp.where(slot >= 6, east_ref[at, :], pack_ref[at, :]))
        edge = by_field(joined)
        one = step(q, edge)
        dx = [pltpu.roll(e, 127, 1) - pltpu.roll(e, 1, 1) for e in edge]
        dy = [
            jnp.where(lane < 24, pltpu.roll(e, 120, 1), 0.0) - jnp.where(lane >= 8, pltpu.roll(e, 8, 1), 0.0)
            for e in edge
        ]
        two = step(one, advanced(coef_ref, 4, edge, dx, dy))
        for r in range(4):
            ref = s_low_ref if r < 2 else s_high_ref
            for f in range(3):
                ref[3 * (r % 2) + f, at, :] = two[r][f]
        return carry

    lax.fori_loop(0, 32, chunk, 0)


def add_side(north, inside, base_ref, half_ref, halo_ref, packs, corner_ref, part_ref, s_ref, coef_ref, spread_ref):
    lane = iota((8, 128), 1)
    sign = (lambda q: q) if north else minus
    near, far = (3, 2) if north else (0, 1)
    spread_ref[...] = spread_corners(corner_ref[...], near)
    set_coefs(coef_ref, 0, [base_ref[4 * k + near:4 * k + near + 1, :] for k in range(4)])
    set_coefs(coef_ref, 1, [base_ref[4 * k + far:4 * k + far + 1, :] for k in range(4)])
    set_coefs(coef_ref, 2, [halo_ref[1536 + k:1537 + k, :] for k in range(4)])
    set_coefs(coef_ref, 3, edge_lines(*packs))

    def chunk(i, carry):
        own = read_row(half_ref, near % 2, i)
        halo = [read_row(halo_ref, k, i) for k in ((0, 1) if north else (1, 0))]
        corner = by_field(spread_ref[eight(i), :])
        dx = [across(lane, halo[0][f], corner[f], near) for f in range(3)]
        dy = sign(plus(halo[1], minus(own)))
        beyond = [x * inside for x in advanced(coef_ref, 2, halo[0], dx, dy)]
        gained = sign(from_north(coef_ref, 0, halo[0]))
        ends = [beside(lane, e) for e in sign(from_north(coef_ref, 3, corner))]
        dx = [across(lane, gained[f], ends[f], near) for f in range(3)]
        first = advanced(coef_ref, 0, gained, dx, sign(beyond))
        second = sign(from_north(coef_ref, 1, gained))
        for f in range(3):
            for r, add in ((near % 2, first), (far % 2, second)):
                s_ref[3 * r + f, eight(i), :] = part_ref[3 * r + f, eight(i), :] + add[f]
        return carry

    lax.fori_loop(0, 32, chunk, 0)


def gram_of(s_ref):
    total = jnp.zeros((256, 256), F32)
    for c in range(0, 6, 2):
        both = jnp.concatenate([s_ref[c], s_ref[c + 1]], axis=1)
        total = total + lax.dot_general(
            both, both, (((1,), (1,)), ((), ())), precision=HI, preferred_element_type=F32
        )
    return total


def south_side(
    inside_ref, base_ref, half_ref, halo_ref, pack_ref, west_ref, east_ref, corner_ref, part_ref,
    s_ref, gram_ref, coef_ref, spread_ref,
):
    add_side(False, inside_ref[0].astype(F32), base_ref, half_ref, halo_ref, (pack_ref, west_ref, east_ref),
             corner_ref, part_ref, s_ref, coef_ref, spread_ref)
    gram_ref[...] = gram_of(s_ref)


def north_side(
    inside_ref, base_ref, half_ref, halo_ref, pack_ref, west_ref, east_ref, corner_ref, part_ref, partial_ref,
    s_ref, gram_ref, coef_ref, spread_ref,
):
    add_side(True, inside_ref[1].astype(F32), base_ref, half_ref, halo_ref, (pack_ref, west_ref, east_ref),
             corner_ref, part_ref, s_ref, coef_ref, spread_ref)
    total = partial_ref[...] + gram_of(s_ref)
    for k, block in enumerate((total[:128, :128], total[128:, :128], total[128:, 128:])):
        for part in range(16):
            lo, hi = max(24 * part, 128 * k), min(24 * part + 24, 128 * k + 128)
            if lo < hi:
                gram_ref[part, lo - 24 * part:hi - 24 * part, :] = block[lo - 128 * k:hi - 128 * k, :]


def sum_copies(in_ref, out_ref):
    total = in_ref[0]
    for k in range(1, in_ref.shape[0]):
        total = total + in_ref[k]
    for k in range(out_ref.shape[0]):
        out_ref[k] = total


def lanes_of(x, lane):
    return jnp.broadcast_to(x[:, lane:lane + 1], x.shape)


def row_of(x, row):
    return jnp.broadcast_to(x[row:row + 1, :], x.shape)


def refined_rsqrt(d):
    r = lax.rsqrt(d)
    return r * (1.5 - 0.5 * d * r * r)


def factor_block(columns):
    e = {(i, m): row_of(columns[m], i) for m in range(8) for i in range(m, 8)}
    w = {}
    low = {}
    for k in range(8):
        r = refined_rsqrt(e[k, k])
        for i in range(k + 1, 8):
            low[i, k] = e[i, k] * r
        for m in range(k + 1, 8):
            for i in range(m, 8):
                e[i, m] = e[i, m] - low[i, k] * low[m, k]
        w[k, k] = r
        for j in range(k):
            acc = low[k, j] * w[j, j]
            for m in range(j + 1, k):
                acc = acc + low[k, m] * w[m, j]
            w[k, j] = -(acc * r)
    return w


def eliminate(m_ref):
    sub = iota((8, 128), 0)
    for panel in range(8):
        j0 = 32 * panel
        td = j0 // 128
        tiles = (0, 1, 2) if td == 0 else (1, 2, 3)
        rows = [{t: m_ref[j0 + 8 * g:j0 + 8 * g + 8, 128 * t:128 * t + 128] for t in tiles} for g in range(4)]
        for b in range(4):
            lane = j0 % 128 + 8 * b
            pivot = rows[b]
            w = factor_block([lanes_of(pivot[td], lane + m) for m in range(8)])
            wcol = []
            for k in range(8):
                c = w[7, k]
                for i in range(6, k - 1, -1):
                    c = jnp.where(sub <= i, w[i, k], c)
                if k:
                    c = jnp.where(sub < k, 0.0, c)
                wcol.append(c)
            done = {}
            for t in tiles:
                acc = wcol[0] * row_of(pivot[t], 0)
                for k in range(1, 8):
                    acc = acc + wcol[k] * row_of(pivot[t], k)
                done[t] = acc
                m_ref[j0 + 8 * b:j0 + 8 * b + 8, 128 * t:128 * t + 128] = acc
            rows[b] = done
            spread = {t: [row_of(done[t], k) for k in range(8)] for t in tiles}
            for g in range(b + 1, 4):
                left = [lanes_of(rows[g][td], lane + m) for m in range(8)]
                coef = []
                for k in range(8):
                    c = w[k, 0] * left[0]
                    for m in range(1, k + 1):
                        c = c + w[k, m] * left[m]
                    coef.append(c)
                for t in tiles:
                    x = rows[g][t]
                    s0 = coef[0] * spread[t][0]
                    s1 = coef[1] * spread[t][1]
                    for k in range(2, 8, 2):
                        s0 = s0 + coef[k] * spread[t][k]
                        s1 = s1 + coef[k + 1] * spread[t][k + 1]
                    rows[g][t] = x - (s0 + s1)
        if panel == 7:
            break
        first = j0 + 32
        top = jnp.concatenate([jnp.concatenate([rows[g][t] for t in tiles], axis=1) for g in range(4)], axis=0)
        for half in range(first // 128, 2):
            col = 128 * (half - td)
            begin = max(first, 128 * half)
            use = top if half == td else top[:, 128:]
            delta = lax.dot_general(top[:, col:col + 128], use, (((0,), (0,)), ((), ())),
                                    precision=HI, preferred_element_type=jnp.float32)
            lo = 128 * tiles[0] if half == td else 128 * tiles[1]
            hi = 128 * (tiles[-1] + 1)
            m_ref[begin:128 * half + 128, lo:hi] = m_ref[begin:128 * half + 128, lo:hi] - delta[begin - 128 * half:, :]


def chol_fields(gram_ref, low_ref, high_ref, out_ref, upper_ref, m_ref, *, cells):
    row = iota((128, 128), 0)
    col = iota((128, 128), 1)
    eye = jnp.where(row == col, 1.0, 0.0).astype(F32)
    blank = jnp.zeros((128, 128), F32)
    scaled = gram_ref[...] * (1.0 / cells)
    m_ref[0:128, 0:128] = scaled[0:128]
    m_ref[128:256, 0:128] = scaled[128:256]
    m_ref[0:128, 128:256] = scaled[128:256].T
    m_ref[128:256, 128:256] = scaled[256:384]
    m_ref[0:128, 256:384] = eye
    m_ref[0:128, 384:512] = blank
    m_ref[128:256, 256:384] = blank
    m_ref[128:256, 384:512] = eye
    eliminate(m_ref)
    upper_ref[0:128, 0:128] = jnp.where(row <= col, m_ref[0:128, 0:128], 0.0)
    upper_ref[0:128, 128:256] = m_ref[0:128, 128:256]
    upper_ref[128:256, 0:128] = blank
    upper_ref[128:256, 128:256] = jnp.where(row <= col, m_ref[128:256, 128:256], 0.0)
    first = jnp.where(row >= col, m_ref[0:128, 256:384], 0.0)
    second = jnp.concatenate([m_ref[128:256, 256:384], jnp.where(row >= col, m_ref[128:256, 384:512], 0.0)], axis=1)
    inverse = jnp.concatenate([jnp.concatenate([first, blank], axis=1), second], axis=0)
    for half, ref in enumerate((low_ref, high_ref)):
        for c in range(0, 6, 2):
            both = jnp.concatenate([ref[c], ref[c + 1]], axis=1)
            y = jnp.dot(inverse, both, precision=HI, preferred_element_type=F32)
            for k in range(2):
                r, f = divmod(c + k, 3)
                out_ref[pl.ds(4 * f + 2 * half + r, 256, stride=12), :] = y[:, 128 * k:128 * k + 128]


def on_chip(*shapes):
    return tuple(pltpu.VMEM(s, F32) for s in shapes)


def kernel(body, out_shape, *args, scratch=(), flags=None):
    args = [pltpu.with_memory_space_constraint(a, pltpu.VMEM) for a in args]
    specs = [pl.BlockSpec(memory_space=pltpu.VMEM)] * len(args)
    if flags is not None:
        args = [flags] + args
        specs = [pl.BlockSpec(memory_space=pltpu.SMEM)] + specs
    out_specs = tuple(pl.BlockSpec(memory_space=pltpu.VMEM) for _ in out_shape)
    return pl.pallas_call(
        body, out_shape=out_shape, in_specs=specs, out_specs=out_specs,
        scratch_shapes=[pltpu.VMEM(s, F32) for s in scratch],
        compiler_params=pltpu.CompilerParams(vmem_limit_bytes=16 * 2**20),
    )(*args)


def per_device(tangent, base_state):
    n_lat = lax.axis_size("lat")
    n_lon = lax.axis_size("lon")
    x = tangent.reshape(3072, 128)
    base = base_state.reshape(16, 128)
    low, high, pack = kernel(split_rows, on_chip((1544, 128), (1544, 128), (264, 128)), x, base)
    east_ring = [(i, (i + 1) % n_lon) for i in range(n_lon)]
    west_ring = [(j, i) for i, j in east_ring]
    north_line = [(i, i + 1) for i in range(n_lat - 1)]
    south_line = [(j, i) for i, j in north_line]
    south = lax.ppermute(high, "lat", north_line)
    north = lax.ppermute(low, "lat", south_line)
    west = lax.ppermute(pack, "lon", east_ring)
    east = lax.ppermute(pack, "lon", west_ring)
    corner_up, corner_down = kernel(corners_out, on_chip((8, 256), (8, 256)), west, east)
    south_corner = lax.ppermute(corner_up, "lat", north_line)
    north_corner = lax.ppermute(corner_down, "lat", south_line)
    part_low, part_high = kernel(
        own_part, on_chip((6, 256, 128), (6, 256, 128)), base, low, high, pack, west, east, scratch=[(20, 8, 128)]
    )
    index = lax.axis_index("lat")
    inside = jnp.stack([index > 0, index < n_lat - 1]).astype(jnp.int32)
    scratch = [(16, 8, 128), (256, 128)]
    s_low, gram = kernel(
        south_side, on_chip((6, 256, 128), (256, 256)),
        base, low, south, pack, west, east, south_corner, part_low, scratch=scratch, flags=inside,
    )
    s_high, gram = kernel(
        north_side, on_chip((6, 256, 128), (16, 24, 128)),
        base, high, north, pack, west, east, north_corner, part_high, gram, scratch=scratch, flags=inside,
    )
    gram = lax.all_to_all(gram, "lon", 0, 0, tiled=True)
    (gram,) = kernel(sum_copies, on_chip((n_lat, 24, 128)), gram)
    gram = lax.all_to_all(gram, "lat", 0, 0, tiled=True)
    (gram,) = kernel(sum_copies, on_chip((n_lon, 24, 128)), gram)
    gram = lax.all_to_all(gram, "lon", 0, 0, tiled=True)
    cells = 4 * 128 * n_lat * n_lon
    fields, upper = kernel(
        lambda *refs: chol_fields(*refs, cells=cells),
        tuple(jax.ShapeDtypeStruct(s, F32) for s in ((3072, 128), (256, 256))),
        gram.reshape(384, 128), s_low, s_high, scratch=[(256, 512)],
    )
    return (fields.reshape(tangent.shape), upper)


def solution(mesh):
    in_specs = (P(None, None, "lat", "lon"), P(None, "lat", "lon"))
    out_specs = (P(None, None, "lat", "lon"), P())
    return jax.shard_map(
        per_device, mesh=mesh, in_specs=in_specs, out_specs=out_specs, check_vma=False
    )
```

```python
import jax
import jax.numpy as jnp
from jax import lax
from jax.experimental import pallas as pl
from jax.experimental.pallas import tpu as pltpu
from jax.sharding import PartitionSpec as P

HI = lax.Precision.HIGHEST
F32 = jnp.float32


def iota(shape, dim):
    return lax.broadcasted_iota(jnp.int32, shape, dim)


def eight(i):
    return pl.ds(pl.multiple_of(8 * i, 8), 8)


def split_rows(x_ref, base_ref, low_ref, high_ref, pack_ref):
    lane = iota((8, 128), 1)
    slot = lane % 32
    field = lane // 32

    def packed(parts):
        acc = jnp.zeros((8, 128), F32)
        for f, r, part in parts:
            at = 32 * f + 8 * r
            moved = pltpu.roll(part, (at + 2) % 128, 1)
            acc = acc + jnp.where((field == f) & (slot >= 8 * r) & (slot < 8 * r + 4), moved, 0.0)
        return acc + pltpu.roll(acc, 4, 1)

    def chunk(i, carry):
        for half in range(2):
            parts = []
            for f in range(3):
                for r in range(4):
                    part = x_ref[pl.ds(192 * i + 96 * half + 4 * f + r, 8, stride=12), :]
                    ref = low_ref if r < 2 else high_ref
                    start = ((r % 2) * 3 + f) * 256
                    ref[pl.ds(pl.multiple_of(start + 16 * i + 8 * half, 8), 8), :] = part
                    parts.append((f, r, part))
            pack_ref[eight(2 * i + half), :] = packed(parts)
        return carry

    lax.fori_loop(0, 16, chunk, 0, unroll=2)
    parts = []
    for r in range(4):
        rows = base_ref[pl.ds(r, 4, stride=4), :]
        both = jnp.concatenate([rows, rows], axis=0)
        parts.append((0, r, both))
        if r == 0:
            low_ref[1536:1544, :] = both
        if r == 3:
            high_ref[1536:1544, :] = both
    pack_ref[256:264, :] = packed(parts)


def corners_out(west_ref, east_ref, up_ref, down_ref):
    slot = iota((256, 128), 1) % 8
    joined = jnp.where(slot < 4, west_ref[0:256, :], east_ref[0:256, :])
    row = iota((8, 128), 0)
    lane = iota((8, 128), 1)
    for ref, r in ((up_ref, 3), (down_ref, 0)):
        at = 32 * (row // 2) + 8 * r + jnp.where(row % 2 == 0, 1, 6)
        pick = jnp.where((lane == at) & (row < 6), 1.0, 0.0)
        ref[...] = lax.dot_general(
            pick, joined, (((1,), (1,)), ((), ())), precision=HI, preferred_element_type=F32
        )


def spread_corners(corner, r):
    row = iota((8, 128), 0)
    lane = iota((8, 128), 1)
    at = 32 * (row // 2) + 8 * r
    west = (row % 2 == 0) & (lane == at + 1)
    east = (row % 2 == 1) & ((lane == at) | (lane == at + 6))
    place = jnp.where((west | east) & (row < 6), 1.0, 0.0)
    return lax.dot_general(
        corner, place, (((0,), (0,)), ((), ())), precision=HI, preferred_element_type=F32
    )


def set_coefs(coef_ref, at, lines):
    for plane, line in enumerate(lines):
        coef_ref[4 * at + plane] = jnp.broadcast_to((1.0 if plane == 3 else 0.5) * line, (8, 128))


def edge_lines(pack_ref, west_ref, east_ref):
    slot = iota((1, 128), 1) % 8
    for plane in range(4):
        row = slice(256 + plane, 257 + plane)
        yield jnp.where(slot < 2, west_ref[row, :], jnp.where(slot >= 6, east_ref[row, :], pack_ref[row, :]))


def advanced(coef_ref, at, q, dx, dy):
    a, b, c, d = (coef_ref[4 * at + k] for k in range(4))
    h = q[0] - a * dx[0] - b * dy[0] - c * (dx[1] + dy[2])
    u = q[1] - a * dx[1] - b * dy[1] + d * q[2] - 0.25 * dx[0]
    v = q[2] - a * dx[2] - b * dy[2] - d * q[1] - 0.25 * dy[0]
    return [h, u, v]


def from_north(coef_ref, at, q):
    b, c = (coef_ref[4 * at + k] for k in (1, 2))
    return [-(b * q[0]) - c * q[2], -(b * q[1]), -(b * q[2]) - 0.25 * q[0]]


def minus(q):
    return [-x for x in q]


def plus(p, q):
    return [x + y for x, y in zip(p, q)]


def across(lane, x, ends, r):
    ends = pltpu.roll(ends, (127 - 8 * r) % 128, 1)
    east = jnp.where(lane == 127, ends, pltpu.roll(x, 127, 1))
    west = jnp.where(lane == 0, ends, pltpu.roll(x, 1, 1))
    return east - west


def beside(lane, edge):
    return jnp.where(lane % 8 == 0, pltpu.roll(edge, 122, 1), edge)


def by_field(x):
    return [x, pltpu.roll(x, 96, 1), pltpu.roll(x, 64, 1)]


def read_row(ref, r, i):
    return [ref[pl.ds(pl.multiple_of((3 * r + f) * 256 + 8 * i, 8), 8), :] for f in range(3)]


def own_part(base_ref, low_ref, high_ref, pack_ref, west_ref, east_ref, s_low_ref, s_high_ref, coef_ref):
    lane = iota((8, 128), 1)
    slot = lane % 8
    for r in range(4):
        set_coefs(coef_ref, r, [base_ref[4 * k + r:4 * k + r + 1, :] for k in range(4)])
    set_coefs(coef_ref, 4, edge_lines(pack_ref, west_ref, east_ref))

    def step(q, edge):
        ends = [beside(lane, e) for e in edge]
        out = []
        for r in range(4):
            dx = [across(lane, q[r][f], ends[f], r) for f in range(3)]
            if r == 0:
                dy = q[1]
            elif r == 3:
                dy = minus(q[2])
            else:
                dy = plus(q[r + 1], minus(q[r - 1]))
            out.append(advanced(coef_ref, r, q[r], dx, dy))
        return out

    def chunk(i, carry):
        q = [read_row(low_ref if r < 2 else high_ref, r % 2, i) for r in range(4)]
        at = eight(i)
        joined = jnp.where(slot < 2, west_ref[at, :], jnp.where(slot >= 6, east_ref[at, :], pack_ref[at, :]))
        edge = by_field(joined)
        one = step(q, edge)
        dx = [pltpu.roll(e, 127, 1) - pltpu.roll(e, 1, 1) for e in edge]
        dy = [
            jnp.where(lane < 24, pltpu.roll(e, 120, 1), 0.0) - jnp.where(lane >= 8, pltpu.roll(e, 8, 1), 0.0)
            for e in edge
        ]
        two = step(one, advanced(coef_ref, 4, edge, dx, dy))
        for r in range(4):
            ref = s_low_ref if r < 2 else s_high_ref
            for f in range(3):
                ref[3 * (r % 2) + f, at, :] = two[r][f]
        return carry

    lax.fori_loop(0, 32, chunk, 0, unroll=2)


def add_side(north, inside, base_ref, half_ref, halo_ref, packs, corner_ref, part_ref, s_ref, coef_ref, spread_ref):
    lane = iota((8, 128), 1)
    sign = (lambda q: q) if north else minus
    near, far = (3, 2) if north else (0, 1)
    spread_ref[...] = spread_corners(corner_ref[...], near)
    set_coefs(coef_ref, 0, [base_ref[4 * k + near:4 * k + near + 1, :] for k in range(4)])
    set_coefs(coef_ref, 1, [base_ref[4 * k + far:4 * k + far + 1, :] for k in range(4)])
    set_coefs(coef_ref, 2, [halo_ref[1536 + k:1537 + k, :] for k in range(4)])
    set_coefs(coef_ref, 3, edge_lines(*packs))

    def chunk(i, carry):
        own = read_row(half_ref, near % 2, i)
        halo = [read_row(halo_ref, k, i) for k in ((0, 1) if north else (1, 0))]
        corner = by_field(spread_ref[eight(i), :])
        dx = [across(lane, halo[0][f], corner[f], near) for f in range(3)]
        dy = sign(plus(halo[1], minus(own)))
        beyond = [x * inside for x in advanced(coef_ref, 2, halo[0], dx, dy)]
        gained = sign(from_north(coef_ref, 0, halo[0]))
        ends = [beside(lane, e) for e in sign(from_north(coef_ref, 3, corner))]
        dx = [across(lane, gained[f], ends[f], near) for f in range(3)]
        first = advanced(coef_ref, 0, gained, dx, sign(beyond))
        second = sign(from_north(coef_ref, 1, gained))
        for f in range(3):
            for r, add in ((near % 2, first), (far % 2, second)):
                s_ref[3 * r + f, eight(i), :] = part_ref[3 * r + f, eight(i), :] + add[f]
        return carry

    lax.fori_loop(0, 32, chunk, 0, unroll=4)


def gram_of(s_ref):
    total = jnp.zeros((256, 256), F32)
    for c in range(0, 6, 2):
        both = jnp.concatenate([s_ref[c], s_ref[c + 1]], axis=1)
        total = total + lax.dot_general(
            both, both, (((1,), (1,)), ((), ())), precision=HI, preferred_element_type=F32
        )
    return total


def south_side(
    inside_ref, base_ref, half_ref, halo_ref, pack_ref, west_ref, east_ref, corner_ref, part_ref,
    s_ref, gram_ref, coef_ref, spread_ref,
):
    add_side(False, inside_ref[0].astype(F32), base_ref, half_ref, halo_ref, (pack_ref, west_ref, east_ref),
             corner_ref, part_ref, s_ref, coef_ref, spread_ref)
    gram_ref[...] = gram_of(s_ref)


def north_side(
    inside_ref, base_ref, half_ref, halo_ref, pack_ref, west_ref, east_ref, corner_ref, part_ref, partial_ref,
    s_ref, gram_ref, coef_ref, spread_ref,
):
    add_side(True, inside_ref[1].astype(F32), base_ref, half_ref, halo_ref, (pack_ref, west_ref, east_ref),
             corner_ref, part_ref, s_ref, coef_ref, spread_ref)
    total = partial_ref[...] + gram_of(s_ref)
    row = iota((128, 128), 0)
    col = iota((128, 128), 1)
    corner = total[128:, 128:]
    gram_ref[0:128, :] = jnp.where(row >= col, total[:128, :128], corner)
    gram_ref[128:256, :] = total[128:, :128]
    diagonal = jnp.sum(jnp.where(row == col, corner, 0.0), axis=0, keepdims=True)
    gram_ref[256:272, :] = jnp.where(iota((16, 128), 0) == 0, diagonal, 0.0)


def sum_copies(in_ref, out_ref):
    total = in_ref[0]
    for k in range(1, in_ref.shape[0]):
        total = total + in_ref[k]
    for k in range(out_ref.shape[0]):
        out_ref[k] = total


def lanes_of(x, lane):
    return jnp.broadcast_to(x[:, lane:lane + 1], x.shape)


def row_of(x, row):
    return jnp.broadcast_to(x[row:row + 1, :], x.shape)


def refined_rsqrt(d):
    r = lax.rsqrt(d)
    return r * (1.5 - 0.5 * d * r * r)


def factor_block(columns):
    e = {(i, m): row_of(columns[m], i) for m in range(8) for i in range(m, 8)}
    w = {}
    low = {}
    for k in range(8):
        r = refined_rsqrt(e[k, k])
        for i in range(k + 1, 8):
            low[i, k] = e[i, k] * r
        for m in range(k + 1, 8):
            for i in range(m, 8):
                e[i, m] = e[i, m] - low[i, k] * low[m, k]
        w[k, k] = r
        for j in range(k):
            acc = low[k, j] * w[j, j]
            for m in range(j + 1, k):
                acc = acc + low[k, m] * w[m, j]
            w[k, j] = -(acc * r)
    return w


def eliminate(m_ref):
    sub = iota((8, 128), 0)
    for panel in range(8):
        j0 = 32 * panel
        td = j0 // 128
        tiles = (0, 1, 2) if td == 0 else (1, 2, 3)
        rows = [{t: m_ref[j0 + 8 * g:j0 + 8 * g + 8, 128 * t:128 * t + 128] for t in tiles} for g in range(4)]
        for b in range(4):
            lane = j0 % 128 + 8 * b
            pivot = rows[b]
            w = factor_block([lanes_of(pivot[td], lane + m) for m in range(8)])
            wcol = []
            for k in range(8):
                c = w[7, k]
                for i in range(6, k - 1, -1):
                    c = jnp.where(sub <= i, w[i, k], c)
                if k:
                    c = jnp.where(sub < k, 0.0, c)
                wcol.append(c)
            done = {}
            for t in tiles:
                acc = wcol[0] * row_of(pivot[t], 0)
                for k in range(1, 8):
                    acc = acc + wcol[k] * row_of(pivot[t], k)
                done[t] = acc
                m_ref[j0 + 8 * b:j0 + 8 * b + 8, 128 * t:128 * t + 128] = acc
            rows[b] = done
            spread = {t: [row_of(done[t], k) for k in range(8)] for t in tiles}
            for g in range(b + 1, 4):
                left = [lanes_of(rows[g][td], lane + m) for m in range(8)]
                coef = []
                for k in range(8):
                    c = w[k, 0] * left[0]
                    for m in range(1, k + 1):
                        c = c + w[k, m] * left[m]
                    coef.append(c)
                for t in tiles:
                    x = rows[g][t]
                    s0 = coef[0] * spread[t][0]
                    s1 = coef[1] * spread[t][1]
                    for k in range(2, 8, 2):
                        s0 = s0 + coef[k] * spread[t][k]
                        s1 = s1 + coef[k + 1] * spread[t][k + 1]
                    rows[g][t] = x - (s0 + s1)
        if panel == 7:
            break
        first = j0 + 32
        top = jnp.concatenate([jnp.concatenate([rows[g][t] for t in tiles], axis=1) for g in range(4)], axis=0)
        for half in range(first // 128, 2):
            col = 128 * (half - td)
            begin = max(first, 128 * half)
            use = top if half == td else top[:, 128:]
            delta = lax.dot_general(top[:, col:col + 128], use, (((0,), (0,)), ((), ())),
                                    precision=HI, preferred_element_type=jnp.float32)
            lo = 128 * tiles[0] if half == td else 128 * tiles[1]
            hi = 128 * (tiles[-1] + 1)
            m_ref[begin:128 * half + 128, lo:hi] = m_ref[begin:128 * half + 128, lo:hi] - delta[begin - 128 * half:, :]


def chol_fields(gram_ref, low_ref, high_ref, out_ref, upper_ref, m_ref, *, cells):
    row = iota((128, 128), 0)
    col = iota((128, 128), 1)
    eye = jnp.where(row == col, 1.0, 0.0).astype(F32)
    blank = jnp.zeros((128, 128), F32)
    packed = gram_ref[...] * (1.0 / cells)
    folded = packed[0:128]
    mirrored = folded.T
    m_ref[0:128, 0:128] = jnp.where(row >= col, folded, mirrored)
    m_ref[128:256, 0:128] = packed[128:256]
    m_ref[0:128, 128:256] = packed[128:256].T
    m_ref[128:256, 128:256] = jnp.where(row < col, folded, jnp.where(row > col, mirrored, packed[256:257]))
    m_ref[0:128, 256:384] = eye
    m_ref[0:128, 384:512] = blank
    m_ref[128:256, 256:384] = blank
    m_ref[128:256, 384:512] = eye
    eliminate(m_ref)
    upper_ref[0:128, 0:128] = jnp.where(row <= col, m_ref[0:128, 0:128], 0.0)
    upper_ref[0:128, 128:256] = m_ref[0:128, 128:256]
    upper_ref[128:256, 0:128] = blank
    upper_ref[128:256, 128:256] = jnp.where(row <= col, m_ref[128:256, 128:256], 0.0)
    first = jnp.where(row >= col, m_ref[0:128, 256:384], 0.0)
    second = jnp.concatenate([m_ref[128:256, 256:384], jnp.where(row >= col, m_ref[128:256, 384:512], 0.0)], axis=1)
    inverse = jnp.concatenate([jnp.concatenate([first, blank], axis=1), second], axis=0)
    for half, ref in enumerate((low_ref, high_ref)):
        for c in range(0, 6, 2):
            both = jnp.concatenate([ref[c], ref[c + 1]], axis=1)
            y = jnp.dot(inverse, both, precision=HI, preferred_element_type=F32)
            for k in range(2):
                r, f = divmod(c + k, 3)
                out_ref[pl.ds(4 * f + 2 * half + r, 256, stride=12), :] = y[:, 128 * k:128 * k + 128]


def on_chip(*shapes):
    return tuple(pltpu.VMEM(s, F32) for s in shapes)


def kernel(body, out_shape, *args, scratch=(), flags=None):
    args = [pltpu.with_memory_space_constraint(a, pltpu.VMEM) for a in args]
    specs = [pl.BlockSpec(memory_space=pltpu.VMEM)] * len(args)
    if flags is not None:
        args = [flags] + args
        specs = [pl.BlockSpec(memory_space=pltpu.SMEM)] + specs
    out_specs = tuple(pl.BlockSpec(memory_space=pltpu.VMEM) for _ in out_shape)
    return pl.pallas_call(
        body, out_shape=out_shape, in_specs=specs, out_specs=out_specs,
        scratch_shapes=[pltpu.VMEM(s, F32) for s in scratch],
        compiler_params=pltpu.CompilerParams(vmem_limit_bytes=16 * 2**20),
    )(*args)


def per_device(tangent, base_state):
    n_lat = lax.axis_size("lat")
    n_lon = lax.axis_size("lon")
    x = tangent.reshape(3072, 128)
    base = base_state.reshape(16, 128)
    low, high, pack = kernel(split_rows, on_chip((1544, 128), (1544, 128), (264, 128)), x, base)
    east_ring = [(i, (i + 1) % n_lon) for i in range(n_lon)]
    west_ring = [(j, i) for i, j in east_ring]
    north_line = [(i, i + 1) for i in range(n_lat - 1)]
    south_line = [(j, i) for i, j in north_line]
    south = lax.ppermute(high, "lat", north_line)
    north = lax.ppermute(low, "lat", south_line)
    west = lax.ppermute(pack, "lon", east_ring)
    east = lax.ppermute(pack, "lon", west_ring)
    corner_up, corner_down = kernel(corners_out, on_chip((8, 256), (8, 256)), west, east)
    south_corner = lax.ppermute(corner_up, "lat", north_line)
    north_corner = lax.ppermute(corner_down, "lat", south_line)
    part_low, part_high = kernel(
        own_part, on_chip((6, 256, 128), (6, 256, 128)), base, low, high, pack, west, east, scratch=[(20, 8, 128)]
    )
    index = lax.axis_index("lat")
    inside = jnp.stack([index > 0, index < n_lat - 1]).astype(jnp.int32)
    scratch = [(16, 8, 128), (256, 128)]
    s_low, gram = kernel(
        south_side, on_chip((6, 256, 128), (256, 256)),
        base, low, south, pack, west, east, south_corner, part_low, scratch=scratch, flags=inside,
    )
    s_high, gram = kernel(
        north_side, on_chip((6, 256, 128), (272, 128)),
        base, high, north, pack, west, east, north_corner, part_high, gram, scratch=scratch, flags=inside,
    )
    gram = lax.all_to_all(gram.reshape(n_lon, 1, -1), "lon", 0, 0, tiled=True)
    (gram,) = kernel(sum_copies, on_chip((n_lat,) + gram.shape[1:]), gram)
    gram = lax.all_to_all(gram, "lat", 0, 0, tiled=True)
    (gram,) = kernel(sum_copies, on_chip((n_lon,) + gram.shape[1:]), gram)
    gram = lax.all_to_all(gram, "lon", 0, 0, tiled=True)
    cells = 4 * 128 * n_lat * n_lon
    fields, upper = kernel(
        lambda *refs: chol_fields(*refs, cells=cells),
        tuple(jax.ShapeDtypeStruct(s, F32) for s in ((3072, 128), (256, 256))),
        gram.reshape(272, 128), s_low, s_high, scratch=[(256, 512)],
    )
    return (fields.reshape(tangent.shape), upper)


def solution(mesh):
    in_specs = (P(None, None, "lat", "lon"), P(None, "lat", "lon"))
    out_specs = (P(None, None, "lat", "lon"), P())
    return jax.shard_map(
        per_device, mesh=mesh, in_specs=in_specs, out_specs=out_specs, check_vma=False
    )
```

```python
import jax
import jax.numpy as jnp
from jax import lax
from jax.experimental import pallas as pl
from jax.experimental.pallas import tpu as pltpu
from jax.sharding import PartitionSpec as P

HI = lax.Precision.HIGHEST
F32 = jnp.float32


def iota(shape, dim):
    return lax.broadcasted_iota(jnp.int32, shape, dim)


def eight(i):
    return pl.ds(pl.multiple_of(8 * i, 8), 8)


def split_rows(x_ref, base_ref, low_ref, high_ref, pack_ref):
    lane = iota((8, 128), 1)
    slot = lane % 32
    field = lane // 32

    def packed(parts):
        acc = jnp.zeros((8, 128), F32)
        for f, r, part in parts:
            at = 32 * f + 8 * r
            moved = pltpu.roll(part, (at + 2) % 128, 1)
            acc = acc + jnp.where((field == f) & (slot >= 8 * r) & (slot < 8 * r + 4), moved, 0.0)
        return acc + pltpu.roll(acc, 4, 1)

    def chunk(i, carry):
        for half in range(2):
            parts = []
            for f in range(3):
                for r in range(4):
                    part = x_ref[pl.ds(192 * i + 96 * half + 4 * f + r, 8, stride=12), :]
                    ref = low_ref if r < 2 else high_ref
                    start = ((r % 2) * 3 + f) * 256
                    ref[pl.ds(pl.multiple_of(start + 16 * i + 8 * half, 8), 8), :] = part
                    parts.append((f, r, part))
            pack_ref[eight(2 * i + half), :] = packed(parts)
        return carry

    lax.fori_loop(0, 16, chunk, 0, unroll=2)
    parts = []
    for r in range(4):
        rows = base_ref[pl.ds(r, 4, stride=4), :]
        both = jnp.concatenate([rows, rows], axis=0)
        parts.append((0, r, both))
        if r == 0:
            low_ref[1536:1544, :] = both
        if r == 3:
            high_ref[1536:1544, :] = both
    pack_ref[256:264, :] = packed(parts)


def corners_out(west_ref, east_ref, up_ref, down_ref):
    slot = iota((256, 128), 1) % 8
    joined = jnp.where(slot < 4, west_ref[0:256, :], east_ref[0:256, :])
    row = iota((8, 128), 0)
    lane = iota((8, 128), 1)
    for ref, r in ((up_ref, 3), (down_ref, 0)):
        at = 32 * (row // 2) + 8 * r + jnp.where(row % 2 == 0, 1, 6)
        pick = jnp.where((lane == at) & (row < 6), 1.0, 0.0)
        ref[...] = lax.dot_general(
            pick, joined, (((1,), (1,)), ((), ())), precision=HI, preferred_element_type=F32
        )


def spread_corners(corner, r):
    row = iota((8, 128), 0)
    lane = iota((8, 128), 1)
    at = 32 * (row // 2) + 8 * r
    west = (row % 2 == 0) & (lane == at + 1)
    east = (row % 2 == 1) & ((lane == at) | (lane == at + 6))
    place = jnp.where((west | east) & (row < 6), 1.0, 0.0)
    return lax.dot_general(
        corner, place, (((0,), (0,)), ((), ())), precision=HI, preferred_element_type=F32
    )


def set_coefs(coef_ref, at, lines):
    for plane, line in enumerate(lines):
        coef_ref[4 * at + plane] = jnp.broadcast_to((1.0 if plane == 3 else 0.5) * line, (8, 128))


def edge_lines(pack_ref, west_ref, east_ref):
    slot = iota((1, 128), 1) % 8
    for plane in range(4):
        row = slice(256 + plane, 257 + plane)
        yield jnp.where(slot < 2, west_ref[row, :], jnp.where(slot >= 6, east_ref[row, :], pack_ref[row, :]))


def advanced(coef_ref, at, q, dx, dy):
    a, b, c, d = (coef_ref[4 * at + k] for k in range(4))
    h = q[0] - a * dx[0] - b * dy[0] - c * (dx[1] + dy[2])
    u = q[1] - a * dx[1] - b * dy[1] + d * q[2] - 0.25 * dx[0]
    v = q[2] - a * dx[2] - b * dy[2] - d * q[1] - 0.25 * dy[0]
    return [h, u, v]


def from_north(coef_ref, at, q):
    b, c = (coef_ref[4 * at + k] for k in (1, 2))
    return [-(b * q[0]) - c * q[2], -(b * q[1]), -(b * q[2]) - 0.25 * q[0]]


def minus(q):
    return [-x for x in q]


def plus(p, q):
    return [x + y for x, y in zip(p, q)]


def across(lane, x, ends, r):
    ends = pltpu.roll(ends, (127 - 8 * r) % 128, 1)
    east = jnp.where(lane == 127, ends, pltpu.roll(x, 127, 1))
    west = jnp.where(lane == 0, ends, pltpu.roll(x, 1, 1))
    return east - west


def beside(lane, edge):
    return jnp.where(lane % 8 == 0, pltpu.roll(edge, 122, 1), edge)


def by_field(x):
    return [x, pltpu.roll(x, 96, 1), pltpu.roll(x, 64, 1)]


def read_row(ref, r, i):
    return [ref[pl.ds(pl.multiple_of((3 * r + f) * 256 + 8 * i, 8), 8), :] for f in range(3)]


def own_part(base_ref, low_ref, high_ref, pack_ref, west_ref, east_ref, s_low_ref, s_high_ref, coef_ref):
    lane = iota((8, 128), 1)
    slot = lane % 8
    for r in range(4):
        set_coefs(coef_ref, r, [base_ref[4 * k + r:4 * k + r + 1, :] for k in range(4)])
    set_coefs(coef_ref, 4, edge_lines(pack_ref, west_ref, east_ref))

    def step(q, edge):
        ends = [beside(lane, e) for e in edge]
        out = []
        for r in range(4):
            dx = [across(lane, q[r][f], ends[f], r) for f in range(3)]
            if r == 0:
                dy = q[1]
            elif r == 3:
                dy = minus(q[2])
            else:
                dy = plus(q[r + 1], minus(q[r - 1]))
            out.append(advanced(coef_ref, r, q[r], dx, dy))
        return out

    def chunk(i, carry):
        q = [read_row(low_ref if r < 2 else high_ref, r % 2, i) for r in range(4)]
        at = eight(i)
        joined = jnp.where(slot < 2, west_ref[at, :], jnp.where(slot >= 6, east_ref[at, :], pack_ref[at, :]))
        edge = by_field(joined)
        one = step(q, edge)
        dx = [pltpu.roll(e, 127, 1) - pltpu.roll(e, 1, 1) for e in edge]
        dy = [
            jnp.where(lane < 24, pltpu.roll(e, 120, 1), 0.0) - jnp.where(lane >= 8, pltpu.roll(e, 8, 1), 0.0)
            for e in edge
        ]
        two = step(one, advanced(coef_ref, 4, edge, dx, dy))
        for r in range(4):
            ref = s_low_ref if r < 2 else s_high_ref
            for f in range(3):
                ref[3 * (r % 2) + f, at, :] = two[r][f]
        return carry

    lax.fori_loop(0, 32, chunk, 0, unroll=2)


def add_side(north, inside, base_ref, half_ref, halo_ref, packs, corner_ref, part_ref, s_ref, coef_ref, spread_ref):
    lane = iota((8, 128), 1)
    sign = (lambda q: q) if north else minus
    near, far = (3, 2) if north else (0, 1)
    spread_ref[...] = spread_corners(corner_ref[...], near)
    set_coefs(coef_ref, 0, [base_ref[4 * k + near:4 * k + near + 1, :] for k in range(4)])
    set_coefs(coef_ref, 1, [base_ref[4 * k + far:4 * k + far + 1, :] for k in range(4)])
    set_coefs(coef_ref, 2, [halo_ref[1536 + k:1537 + k, :] for k in range(4)])
    set_coefs(coef_ref, 3, edge_lines(*packs))

    def chunk(i, carry):
        own = read_row(half_ref, near % 2, i)
        halo = [read_row(halo_ref, k, i) for k in ((0, 1) if north else (1, 0))]
        corner = by_field(spread_ref[eight(i), :])
        dx = [across(lane, halo[0][f], corner[f], near) for f in range(3)]
        dy = sign(plus(halo[1], minus(own)))
        beyond = [x * inside for x in advanced(coef_ref, 2, halo[0], dx, dy)]
        gained = sign(from_north(coef_ref, 0, halo[0]))
        ends = [beside(lane, e) for e in sign(from_north(coef_ref, 3, corner))]
        dx = [across(lane, gained[f], ends[f], near) for f in range(3)]
        first = advanced(coef_ref, 0, gained, dx, sign(beyond))
        second = sign(from_north(coef_ref, 1, gained))
        for f in range(3):
            for r, add in ((near % 2, first), (far % 2, second)):
                s_ref[3 * r + f, eight(i), :] = part_ref[3 * r + f, eight(i), :] + add[f]
        return carry

    lax.fori_loop(0, 32, chunk, 0, unroll=4)


def gram_of(s_ref):
    total = jnp.zeros((256, 256), F32)
    for c in range(0, 6, 2):
        both = jnp.concatenate([s_ref[c], s_ref[c + 1]], axis=1)
        total = total + lax.dot_general(
            both, both, (((1,), (1,)), ((), ())), precision=HI, preferred_element_type=F32
        )
    return total


def south_side(
    inside_ref, base_ref, half_ref, halo_ref, pack_ref, west_ref, east_ref, corner_ref, part_ref,
    s_ref, gram_ref, coef_ref, spread_ref,
):
    add_side(False, inside_ref[0].astype(F32), base_ref, half_ref, halo_ref, (pack_ref, west_ref, east_ref),
             corner_ref, part_ref, s_ref, coef_ref, spread_ref)
    gram_ref[...] = gram_of(s_ref)


def north_side(
    inside_ref, base_ref, half_ref, halo_ref, pack_ref, west_ref, east_ref, corner_ref, part_ref, partial_ref,
    s_ref, gram_ref, coef_ref, spread_ref,
):
    add_side(True, inside_ref[1].astype(F32), base_ref, half_ref, halo_ref, (pack_ref, west_ref, east_ref),
             corner_ref, part_ref, s_ref, coef_ref, spread_ref)
    total = partial_ref[...] + gram_of(s_ref)
    row = iota((128, 128), 0)
    col = iota((128, 128), 1)
    corner = total[128:, 128:]
    gram_ref[0:128, :] = jnp.where(row >= col, total[:128, :128], corner)
    gram_ref[128:256, :] = total[128:, :128]
    diagonal = jnp.sum(jnp.where(row == col, corner, 0.0), axis=0, keepdims=True)
    gram_ref[256:272, :] = jnp.where(iota((16, 128), 0) == 0, diagonal, 0.0)


def sum_copies(in_ref, out_ref):
    total = in_ref[0]
    for k in range(1, in_ref.shape[0]):
        total = total + in_ref[k]
    for k in range(out_ref.shape[0]):
        out_ref[k] = total


def lanes_of(x, lane):
    return jnp.broadcast_to(x[:, lane:lane + 1], x.shape)


def row_of(x, row):
    return jnp.broadcast_to(x[row:row + 1, :], x.shape)


def eliminate(m_ref):
    sub = iota((8, 128), 0)
    for panel in range(4):
        j0 = 64 * panel
        td = j0 // 128
        tiles = (0, 1, 2) if td == 0 else (1, 2, 3)
        rows = [{t: m_ref[j0 + 8 * g:j0 + 8 * g + 8, 128 * t:128 * t + 128] for t in tiles} for g in range(8)]
        for b in range(8):
            lane = j0 % 128 + 8 * b
            cols = [[lanes_of(rows[b][td], lane + m) for m in range(8)]]
            work = [dict(rows[g]) for g in range(b, 8)]
            pivot = row_of(cols[0][0], 0)
            steps = []
            for k in range(8):
                r = lax.rsqrt(pivot)
                inv = r * r
                scale = r if k == 0 else jnp.where(sub == k, r, scale)
                line = {m: row_of(cols[0][m], k) for m in range(k + 1, 8)}
                if k < 7:
                    pivot = row_of(cols[0][k + 1], k + 1) - (line[k + 1] * line[k + 1]) * inv
                wide = {t: row_of(work[0][t], k) for t in tiles}
                f = jnp.where(sub > k, cols[0][k] * inv, 0.0)
                for m in range(k + 1, 8):
                    cols[0][m] = cols[0][m] - f * line[m]
                for t in tiles:
                    work[0][t] = work[0][t] - f * wide[t]
                steps.append((inv, line, wide))
            for g in range(1, 8 - b):
                left = [lanes_of(rows[b + g][td], lane + m) for m in range(8)]
                for k, (inv, line, wide) in enumerate(steps):
                    f = left[k] * inv
                    for m in range(k + 1, 8):
                        left[m] = left[m] - f * line[m]
                    for t in tiles:
                        work[g][t] = work[g][t] - f * wide[t]
            for g in range(b, 8):
                rows[g] = work[g - b]
            for t in tiles:
                rows[b][t] = rows[b][t] * scale
                m_ref[j0 + 8 * b:j0 + 8 * b + 8, 128 * t:128 * t + 128] = rows[b][t]
        if panel == 3:
            break
        first = j0 + 64
        top = jnp.concatenate([jnp.concatenate([rows[g][t] for t in tiles], axis=1) for g in range(8)], axis=0)
        spans = []
        for half in range(first // 128, 2):
            begin = max(first, 128 * half)
            end = 128 * half + 128
            if begin == first and True:
                spans.append((half, begin, begin + 64))
                begin += 64
            if begin < end:
                spans.append((half, begin, end))
        turned = {half: top[:, 128 * (half - td):128 * (half - td) + 128].T for half in range(first // 128, 2)}
        for half, begin, end in spans:
            use = top if half == td else top[:, 128:]
            delta = jnp.dot(turned[half][begin - 128 * half:end - 128 * half, :], use, precision=HI, preferred_element_type=F32)
            lo = 128 * tiles[0] if half == td else 128 * tiles[1]
            hi = 128 * (tiles[-1] + 1)
            m_ref[begin:end, lo:hi] = m_ref[begin:end, lo:hi] - delta


def chol_fields(gram_ref, low_ref, high_ref, out_ref, upper_ref, m_ref, *, cells):
    row = iota((128, 128), 0)
    col = iota((128, 128), 1)
    eye = jnp.where(row == col, 1.0, 0.0).astype(F32)
    blank = jnp.zeros((128, 128), F32)
    packed = gram_ref[...] * (1.0 / cells)
    folded = packed[0:128]
    mirrored = folded.T
    m_ref[0:128, 0:128] = jnp.where(row >= col, folded, mirrored)
    m_ref[128:256, 0:128] = packed[128:256]
    m_ref[0:128, 128:256] = packed[128:256].T
    m_ref[128:256, 128:256] = jnp.where(row < col, folded, jnp.where(row > col, mirrored, packed[256:257]))
    m_ref[0:128, 256:384] = eye
    m_ref[0:128, 384:512] = blank
    m_ref[128:256, 256:384] = blank
    m_ref[128:256, 384:512] = eye
    eliminate(m_ref)
    upper_ref[0:128, 0:128] = jnp.where(row <= col, m_ref[0:128, 0:128], 0.0)
    upper_ref[0:128, 128:256] = m_ref[0:128, 128:256]
    upper_ref[128:256, 0:128] = blank
    upper_ref[128:256, 128:256] = jnp.where(row <= col, m_ref[128:256, 128:256], 0.0)
    first = jnp.where(row >= col, m_ref[0:128, 256:384], 0.0)
    second = jnp.concatenate([m_ref[128:256, 256:384], jnp.where(row >= col, m_ref[128:256, 384:512], 0.0)], axis=1)
    inverse = jnp.concatenate([jnp.concatenate([first, blank], axis=1), second], axis=0)
    for half, ref in enumerate((low_ref, high_ref)):
        for c in range(0, 6, 2):
            both = jnp.concatenate([ref[c], ref[c + 1]], axis=1)
            y = jnp.dot(inverse, both, precision=HI, preferred_element_type=F32)
            for k in range(2):
                r, f = divmod(c + k, 3)
                out_ref[pl.ds(4 * f + 2 * half + r, 256, stride=12), :] = y[:, 128 * k:128 * k + 128]


def on_chip(*shapes):
    return tuple(pltpu.VMEM(s, F32) for s in shapes)


def kernel(body, out_shape, *args, scratch=(), flags=None):
    args = [pltpu.with_memory_space_constraint(a, pltpu.VMEM) for a in args]
    specs = [pl.BlockSpec(memory_space=pltpu.VMEM)] * len(args)
    if flags is not None:
        args = [flags] + args
        specs = [pl.BlockSpec(memory_space=pltpu.SMEM)] + specs
    out_specs = tuple(pl.BlockSpec(memory_space=pltpu.VMEM) for _ in out_shape)
    return pl.pallas_call(
        body, out_shape=out_shape, in_specs=specs, out_specs=out_specs,
        scratch_shapes=[pltpu.VMEM(s, F32) for s in scratch],
        compiler_params=pltpu.CompilerParams(vmem_limit_bytes=16 * 2**20),
    )(*args)


def per_device(tangent, base_state):
    n_lat = lax.axis_size("lat")
    n_lon = lax.axis_size("lon")
    x = tangent.reshape(3072, 128)
    base = base_state.reshape(16, 128)
    low, high, pack = kernel(split_rows, on_chip((1544, 128), (1544, 128), (264, 128)), x, base)
    east_ring = [(i, (i + 1) % n_lon) for i in range(n_lon)]
    west_ring = [(j, i) for i, j in east_ring]
    north_line = [(i, i + 1) for i in range(n_lat - 1)]
    south_line = [(j, i) for i, j in north_line]
    south = lax.ppermute(high, "lat", north_line)
    north = lax.ppermute(low, "lat", south_line)
    west = lax.ppermute(pack, "lon", east_ring)
    east = lax.ppermute(pack, "lon", west_ring)
    corner_up, corner_down = kernel(corners_out, on_chip((8, 256), (8, 256)), west, east)
    south_corner = lax.ppermute(corner_up, "lat", north_line)
    north_corner = lax.ppermute(corner_down, "lat", south_line)
    part_low, part_high = kernel(
        own_part, on_chip((6, 256, 128), (6, 256, 128)), base, low, high, pack, west, east, scratch=[(20, 8, 128)]
    )
    index = lax.axis_index("lat")
    inside = jnp.stack([index > 0, index < n_lat - 1]).astype(jnp.int32)
    scratch = [(16, 8, 128), (256, 128)]
    s_low, gram = kernel(
        south_side, on_chip((6, 256, 128), (256, 256)),
        base, low, south, pack, west, east, south_corner, part_low, scratch=scratch, flags=inside,
    )
    s_high, gram = kernel(
        north_side, on_chip((6, 256, 128), (272, 128)),
        base, high, north, pack, west, east, north_corner, part_high, gram, scratch=scratch, flags=inside,
    )
    gram = lax.all_to_all(gram.reshape(n_lon, 1, -1), "lon", 0, 0, tiled=True)
    (gram,) = kernel(sum_copies, on_chip((n_lat,) + gram.shape[1:]), gram)
    gram = lax.all_to_all(gram, "lat", 0, 0, tiled=True)
    (gram,) = kernel(sum_copies, on_chip((n_lon,) + gram.shape[1:]), gram)
    gram = lax.all_to_all(gram, "lon", 0, 0, tiled=True)
    cells = 4 * 128 * n_lat * n_lon
    fields, upper = kernel(
        lambda *refs: chol_fields(*refs, cells=cells),
        tuple(jax.ShapeDtypeStruct(s, F32) for s in ((3072, 128), (256, 256))),
        gram.reshape(272, 128), s_low, s_high, scratch=[(256, 512)],
    )
    return (fields.reshape(tangent.shape), upper)


def solution(mesh):
    in_specs = (P(None, None, "lat", "lon"), P(None, "lat", "lon"))
    out_specs = (P(None, None, "lat", "lon"), P())
    return jax.shard_map(
        per_device, mesh=mesh, in_specs=in_specs, out_specs=out_specs, check_vma=False
    )
```

```python
import jax
import jax.numpy as jnp
from jax import lax
from jax.experimental import pallas as pl
from jax.experimental.pallas import tpu as pltpu
from jax.sharding import PartitionSpec as P

HI = lax.Precision.HIGHEST
F32 = jnp.float32


def iota(shape, dim):
    return lax.broadcasted_iota(jnp.int32, shape, dim)


def eight(i):
    return pl.ds(pl.multiple_of(8 * i, 8), 8)


def split_rows(x_hbm, base_hbm, low_ref, high_ref, pack_ref, x_ref, base_ref, sems):
    places = [pl.ds(768 * k, 768) for k in range(4)]
    copies = [pltpu.make_async_copy(x_hbm.at[p], x_ref.at[p], sems.at[k]) for k, p in enumerate(places)]
    base_copy = pltpu.make_async_copy(base_hbm, base_ref, sems.at[4])
    for copy in copies:
        copy.start()
    base_copy.start()
    lane = iota((8, 128), 1)
    slot = lane % 32
    field = lane // 32

    def packed(parts):
        acc = jnp.zeros((8, 128), F32)
        for f, r, part in parts:
            at = 32 * f + 8 * r
            moved = pltpu.roll(part, (at + 2) % 128, 1)
            acc = acc + jnp.where((field == f) & (slot >= 8 * r) & (slot < 8 * r + 4), moved, 0.0)
        return acc + pltpu.roll(acc, 4, 1)

    def chunk(i, carry):
        for half in range(2):
            parts = []
            for f in range(3):
                for r in range(4):
                    part = x_ref[pl.ds(192 * i + 96 * half + 4 * f + r, 8, stride=12), :]
                    ref = low_ref if r < 2 else high_ref
                    start = ((r % 2) * 3 + f) * 256
                    ref[pl.ds(pl.multiple_of(start + 16 * i + 8 * half, 8), 8), :] = part
                    parts.append((f, r, part))
            pack_ref[eight(2 * i + half), :] = packed(parts)
        return carry

    for k, copy in enumerate(copies):
        copy.wait()
        lax.fori_loop(4 * k, 4 * k + 4, chunk, 0, unroll=2)
    base_copy.wait()
    parts = []
    for r in range(4):
        rows = base_ref[pl.ds(r, 4, stride=4), :]
        both = jnp.concatenate([rows, rows], axis=0)
        parts.append((0, r, both))
        if r == 0:
            low_ref[1536:1544, :] = both
        if r == 3:
            high_ref[1536:1544, :] = both
    pack_ref[256:264, :] = packed(parts)


def corners_out(west_ref, east_ref, up_ref, down_ref):
    slot = iota((256, 128), 1) % 8
    joined = jnp.where(slot < 4, west_ref[0:256, :], east_ref[0:256, :])
    row = iota((8, 128), 0)
    lane = iota((8, 128), 1)
    for ref, r in ((up_ref, 3), (down_ref, 0)):
        at = 32 * (row // 2) + 8 * r + jnp.where(row % 2 == 0, 1, 6)
        pick = jnp.where((lane == at) & (row < 6), 1.0, 0.0)
        ref[...] = lax.dot_general(
            pick, joined, (((1,), (1,)), ((), ())), precision=HI, preferred_element_type=F32
        )


def spread_corners(corner, r):
    row = iota((8, 128), 0)
    lane = iota((8, 128), 1)
    at = 32 * (row // 2) + 8 * r
    west = (row % 2 == 0) & (lane == at + 1)
    east = (row % 2 == 1) & ((lane == at) | (lane == at + 6))
    place = jnp.where((west | east) & (row < 6), 1.0, 0.0)
    return lax.dot_general(
        corner, place, (((0,), (0,)), ((), ())), precision=HI, preferred_element_type=F32
    )


def set_coefs(coef_ref, at, lines):
    for plane, line in enumerate(lines):
        coef_ref[4 * at + plane] = jnp.broadcast_to((1.0 if plane == 3 else 0.5) * line, (8, 128))


def edge_lines(pack_ref, west_ref, east_ref):
    slot = iota((1, 128), 1) % 8
    for plane in range(4):
        row = slice(256 + plane, 257 + plane)
        yield jnp.where(slot < 2, west_ref[row, :], jnp.where(slot >= 6, east_ref[row, :], pack_ref[row, :]))


def advanced(coef_ref, at, q, dx, dy):
    a, b, c, d = (coef_ref[4 * at + k] for k in range(4))
    h = q[0] - a * dx[0] - b * dy[0] - c * (dx[1] + dy[2])
    u = q[1] - a * dx[1] - b * dy[1] + d * q[2] - 0.25 * dx[0]
    v = q[2] - a * dx[2] - b * dy[2] - d * q[1] - 0.25 * dy[0]
    return [h, u, v]


def from_north(coef_ref, at, q):
    b, c = (coef_ref[4 * at + k] for k in (1, 2))
    return [-(b * q[0]) - c * q[2], -(b * q[1]), -(b * q[2]) - 0.25 * q[0]]


def minus(q):
    return [-x for x in q]


def plus(p, q):
    return [x + y for x, y in zip(p, q)]


def across(lane, x, ends, r):
    ends = pltpu.roll(ends, (127 - 8 * r) % 128, 1)
    east = jnp.where(lane == 127, ends, pltpu.roll(x, 127, 1))
    west = jnp.where(lane == 0, ends, pltpu.roll(x, 1, 1))
    return east - west


def beside(lane, edge):
    return jnp.where(lane % 8 == 0, pltpu.roll(edge, 122, 1), edge)


def by_field(x):
    return [x, pltpu.roll(x, 96, 1), pltpu.roll(x, 64, 1)]


def read_row(ref, r, i):
    return [ref[pl.ds(pl.multiple_of((3 * r + f) * 256 + 8 * i, 8), 8), :] for f in range(3)]


def own_part(
    base_ref, low_ref, high_ref, pack_ref, west_ref, east_ref, s_low_ref, s_high_ref, coef_ref, one_ref, ends_ref
):
    lane = iota((8, 128), 1)
    slot = lane % 8
    for r in range(4):
        set_coefs(coef_ref, r, [base_ref[4 * k + r:4 * k + r + 1, :] for k in range(4)])
    set_coefs(coef_ref, 4, edge_lines(pack_ref, west_ref, east_ref))

    def step(q, ends):
        out = []
        for r in range(4):
            dx = [across(lane, q[r][f], ends[f], r) for f in range(3)]
            if r == 0:
                dy = q[1]
            elif r == 3:
                dy = minus(q[2])
            else:
                dy = plus(q[r + 1], minus(q[r - 1]))
            out.append(advanced(coef_ref, r, q[r], dx, dy))
        return out

    def first(i, carry):
        q = [read_row(low_ref if r < 2 else high_ref, r % 2, i) for r in range(4)]
        at = eight(i)
        joined = jnp.where(slot < 2, west_ref[at, :], jnp.where(slot >= 6, east_ref[at, :], pack_ref[at, :]))
        edge = by_field(joined)
        one = step(q, [beside(lane, e) for e in edge])
        for r in range(4):
            for f in range(3):
                one_ref[3 * r + f, at, :] = one[r][f]
        dx = [pltpu.roll(e, 127, 1) - pltpu.roll(e, 1, 1) for e in edge]
        dy = [
            jnp.where(lane < 24, pltpu.roll(e, 120, 1), 0.0) - jnp.where(lane >= 8, pltpu.roll(e, 8, 1), 0.0)
            for e in edge
        ]
        for f, e in enumerate(advanced(coef_ref, 4, edge, dx, dy)):
            ends_ref[f, at, :] = beside(lane, e)
        return carry

    def second(i, carry):
        at = eight(i)
        one = [[one_ref[3 * r + f, at, :] for f in range(3)] for r in range(4)]
        two = step(one, [ends_ref[f, at, :] for f in range(3)])
        for r in range(4):
            ref = s_low_ref if r < 2 else s_high_ref
            for f in range(3):
                ref[3 * (r % 2) + f, at, :] = two[r][f]
        return carry

    lax.fori_loop(0, 32, first, 0, unroll=2)
    lax.fori_loop(0, 32, second, 0, unroll=8)


def add_side(north, inside, base_ref, half_ref, halo_ref, packs, corner_ref, part_ref, s_ref, coef_ref, spread_ref):
    lane = iota((8, 128), 1)
    sign = (lambda q: q) if north else minus
    near, far = (3, 2) if north else (0, 1)
    spread_ref[...] = spread_corners(corner_ref[...], near)
    set_coefs(coef_ref, 0, [base_ref[4 * k + near:4 * k + near + 1, :] for k in range(4)])
    set_coefs(coef_ref, 1, [base_ref[4 * k + far:4 * k + far + 1, :] for k in range(4)])
    set_coefs(coef_ref, 2, [halo_ref[1536 + k:1537 + k, :] for k in range(4)])
    set_coefs(coef_ref, 3, edge_lines(*packs))

    def chunk(i, carry):
        own = read_row(half_ref, near % 2, i)
        halo = [read_row(halo_ref, k, i) for k in ((0, 1) if north else (1, 0))]
        corner = by_field(spread_ref[eight(i), :])
        dx = [across(lane, halo[0][f], corner[f], near) for f in range(3)]
        dy = sign(plus(halo[1], minus(own)))
        beyond = [x * inside for x in advanced(coef_ref, 2, halo[0], dx, dy)]
        gained = sign(from_north(coef_ref, 0, halo[0]))
        ends = [beside(lane, e) for e in sign(from_north(coef_ref, 3, corner))]
        dx = [across(lane, gained[f], ends[f], near) for f in range(3)]
        first = advanced(coef_ref, 0, gained, dx, sign(beyond))
        second = sign(from_north(coef_ref, 1, gained))
        for f in range(3):
            for r, add in ((near % 2, first), (far % 2, second)):
                s_ref[3 * r + f, eight(i), :] = part_ref[3 * r + f, eight(i), :] + add[f]
        return carry

    lax.fori_loop(0, 32, chunk, 0, unroll=4)


def gram_of(s_ref):
    total = jnp.zeros((256, 256), F32)
    for c in range(0, 6, 2):
        both = jnp.concatenate([s_ref[c], s_ref[c + 1]], axis=1)
        total = total + lax.dot_general(
            both, both, (((1,), (1,)), ((), ())), precision=HI, preferred_element_type=F32
        )
    return total


def south_side(
    inside_ref, base_ref, half_ref, halo_ref, pack_ref, west_ref, east_ref, corner_ref, part_ref,
    s_ref, gram_ref, coef_ref, spread_ref,
):
    add_side(False, inside_ref[0].astype(F32), base_ref, half_ref, halo_ref, (pack_ref, west_ref, east_ref),
             corner_ref, part_ref, s_ref, coef_ref, spread_ref)
    gram_ref[...] = gram_of(s_ref)


def north_side(
    inside_ref, base_ref, half_ref, halo_ref, pack_ref, west_ref, east_ref, corner_ref, part_ref, partial_ref,
    s_ref, gram_ref, coef_ref, spread_ref,
):
    add_side(True, inside_ref[1].astype(F32), base_ref, half_ref, halo_ref, (pack_ref, west_ref, east_ref),
             corner_ref, part_ref, s_ref, coef_ref, spread_ref)
    total = partial_ref[...] + gram_of(s_ref)
    row = iota((128, 128), 0)
    col = iota((128, 128), 1)
    corner = total[128:, 128:]
    gram_ref[0:128, :] = jnp.where(row >= col, total[:128, :128], corner)
    gram_ref[128:256, :] = total[128:, :128]
    diagonal = jnp.sum(jnp.where(row == col, corner, 0.0), axis=0, keepdims=True)
    gram_ref[256:272, :] = jnp.where(iota((16, 128), 0) == 0, diagonal, 0.0)


def sum_copies(in_ref, out_ref):
    total = in_ref[0]
    for k in range(1, in_ref.shape[0]):
        total = total + in_ref[k]
    for k in range(out_ref.shape[0]):
        out_ref[k] = total


def lanes_of(x, lane):
    return jnp.broadcast_to(x[:, lane:lane + 1], x.shape)


def row_of(x, row):
    return jnp.broadcast_to(x[row:row + 1, :], x.shape)


def eliminate(m_ref):
    sub = iota((8, 128), 0)
    for panel in range(4):
        j0 = 64 * panel
        td = j0 // 128
        tiles = (0, 1, 2) if td == 0 else (1, 2, 3)
        rows = [{t: m_ref[j0 + 8 * g:j0 + 8 * g + 8, 128 * t:128 * t + 128] for t in tiles} for g in range(8)]
        for b in range(8):
            lane = j0 % 128 + 8 * b
            cols = [[lanes_of(rows[b][td], lane + m) for m in range(8)]]
            work = [dict(rows[g]) for g in range(b, 8)]
            pivot = row_of(cols[0][0], 0)
            steps = []
            for k in range(8):
                r = lax.rsqrt(pivot)
                inv = r * r
                scale = r if k == 0 else jnp.where(sub == k, r, scale)
                line = {m: row_of(cols[0][m], k) for m in range(k + 1, 8)}
                if k < 7:
                    pivot = row_of(cols[0][k + 1], k + 1) - (line[k + 1] * line[k + 1]) * inv
                wide = {t: row_of(work[0][t], k) for t in tiles}
                f = jnp.where(sub > k, cols[0][k] * inv, 0.0)
                for m in range(k + 1, 8):
                    cols[0][m] = cols[0][m] - f * line[m]
                for t in tiles:
                    work[0][t] = work[0][t] - f * wide[t]
                steps.append((inv, line, wide))
            for g in range(1, 8 - b):
                left = [lanes_of(rows[b + g][td], lane + m) for m in range(8)]
                for k, (inv, line, wide) in enumerate(steps):
                    f = left[k] * inv
                    for m in range(k + 1, 8):
                        left[m] = left[m] - f * line[m]
                    for t in tiles:
                        work[g][t] = work[g][t] - f * wide[t]
            for g in range(b, 8):
                rows[g] = work[g - b]
            for t in tiles:
                rows[b][t] = rows[b][t] * scale
                m_ref[j0 + 8 * b:j0 + 8 * b + 8, 128 * t:128 * t + 128] = rows[b][t]
        if panel == 3:
            break
        first = j0 + 64
        top = jnp.concatenate([jnp.concatenate([rows[g][t] for t in tiles], axis=1) for g in range(8)], axis=0)
        spans = []
        for half in range(first // 128, 2):
            begin = max(first, 128 * half)
            end = 128 * half + 128
            if begin == first and True:
                spans.append((half, begin, begin + 64))
                begin += 64
            if begin < end:
                spans.append((half, begin, end))
        turned = {half: top[:, 128 * (half - td):128 * (half - td) + 128].T for half in range(first // 128, 2)}
        for half, begin, end in spans:
            use = top if half == td else top[:, 128:]
            delta = jnp.dot(turned[half][begin - 128 * half:end - 128 * half, :], use, precision=HI, preferred_element_type=F32)
            lo = 128 * tiles[0] if half == td else 128 * tiles[1]
            hi = 128 * (tiles[-1] + 1)
            m_ref[begin:end, lo:hi] = m_ref[begin:end, lo:hi] - delta


def chol_fields(gram_ref, low_ref, high_ref, out_ref, upper_ref, m_ref, *, cells):
    row = iota((128, 128), 0)
    col = iota((128, 128), 1)
    eye = jnp.where(row == col, 1.0, 0.0).astype(F32)
    blank = jnp.zeros((128, 128), F32)
    packed = gram_ref[...] * (1.0 / cells)
    folded = packed[0:128]
    mirrored = folded.T
    m_ref[0:128, 0:128] = jnp.where(row >= col, folded, mirrored)
    m_ref[128:256, 0:128] = packed[128:256]
    m_ref[0:128, 128:256] = packed[128:256].T
    m_ref[128:256, 128:256] = jnp.where(row < col, folded, jnp.where(row > col, mirrored, packed[256:257]))
    m_ref[0:128, 256:384] = eye
    m_ref[0:128, 384:512] = blank
    m_ref[128:256, 256:384] = blank
    m_ref[128:256, 384:512] = eye
    eliminate(m_ref)
    upper_ref[0:128, 0:128] = jnp.where(row <= col, m_ref[0:128, 0:128], 0.0)
    upper_ref[0:128, 128:256] = m_ref[0:128, 128:256]
    upper_ref[128:256, 0:128] = blank
    upper_ref[128:256, 128:256] = jnp.where(row <= col, m_ref[128:256, 128:256], 0.0)
    first = jnp.where(row >= col, m_ref[0:128, 256:384], 0.0)
    second = jnp.concatenate([m_ref[128:256, 256:384], jnp.where(row >= col, m_ref[128:256, 384:512], 0.0)], axis=1)
    inverse = jnp.concatenate([jnp.concatenate([first, blank], axis=1), second], axis=0)
    for half, ref in enumerate((low_ref, high_ref)):
        for c in range(0, 6, 2):
            both = jnp.concatenate([ref[c], ref[c + 1]], axis=1)
            y = jnp.dot(inverse, both, precision=HI, preferred_element_type=F32)
            for k in range(2):
                r, f = divmod(c + k, 3)
                out_ref[pl.ds(4 * f + 2 * half + r, 256, stride=12), :] = y[:, 128 * k:128 * k + 128]


def on_chip(*shapes):
    return tuple(pltpu.VMEM(s, F32) for s in shapes)


def kernel(body, out_shape, *args, scratch=(), flags=None):
    args = [pltpu.with_memory_space_constraint(a, pltpu.VMEM) for a in args]
    specs = [pl.BlockSpec(memory_space=pltpu.VMEM)] * len(args)
    if flags is not None:
        args = [flags] + args
        specs = [pl.BlockSpec(memory_space=pltpu.SMEM)] + specs
    out_specs = tuple(pl.BlockSpec(memory_space=pltpu.VMEM) for _ in out_shape)
    return pl.pallas_call(
        body, out_shape=out_shape, in_specs=specs, out_specs=out_specs,
        scratch_shapes=[pltpu.VMEM(s, F32) for s in scratch],
        compiler_params=pltpu.CompilerParams(vmem_limit_bytes=16 * 2**20),
    )(*args)


def per_device(tangent, base_state):
    n_lat = lax.axis_size("lat")
    n_lon = lax.axis_size("lon")
    x = tangent.reshape(3072, 128)
    base = base_state.reshape(16, 128)
    low, high, pack = pl.pallas_call(
        split_rows, out_shape=on_chip((1544, 128), (1544, 128), (264, 128)),
        in_specs=[pl.BlockSpec(memory_space=pl.ANY)] * 2,
        out_specs=(pl.BlockSpec(memory_space=pltpu.VMEM),) * 3,
        scratch_shapes=[pltpu.VMEM((3072, 128), F32), pltpu.VMEM((16, 128), F32), pltpu.SemaphoreType.DMA((5,))],
        compiler_params=pltpu.CompilerParams(vmem_limit_bytes=16 * 2**20),
    )(*[pltpu.with_memory_space_constraint(a, pltpu.HBM) for a in (x, base)])
    east_ring = [(i, (i + 1) % n_lon) for i in range(n_lon)]
    west_ring = [(j, i) for i, j in east_ring]
    north_line = [(i, i + 1) for i in range(n_lat - 1)]
    south_line = [(j, i) for i, j in north_line]
    south = lax.ppermute(high, "lat", north_line)
    north = lax.ppermute(low, "lat", south_line)
    west = lax.ppermute(pack, "lon", east_ring)
    east = lax.ppermute(pack, "lon", west_ring)
    corner_up, corner_down = kernel(corners_out, on_chip((8, 256), (8, 256)), west, east)
    south_corner = lax.ppermute(corner_up, "lat", north_line)
    north_corner = lax.ppermute(corner_down, "lat", south_line)
    part_low, part_high = kernel(
        own_part, on_chip((6, 256, 128), (6, 256, 128)), base, low, high, pack, west, east, scratch=[(20, 8, 128), (12, 256, 128), (3, 256, 128)]
    )
    index = lax.axis_index("lat")
    inside = jnp.stack([index > 0, index < n_lat - 1]).astype(jnp.int32)
    scratch = [(16, 8, 128), (256, 128)]
    s_low, gram = kernel(
        south_side, on_chip((6, 256, 128), (256, 256)),
        base, low, south, pack, west, east, south_corner, part_low, scratch=scratch, flags=inside,
    )
    s_high, gram = kernel(
        north_side, on_chip((6, 256, 128), (272, 128)),
        base, high, north, pack, west, east, north_corner, part_high, gram, scratch=scratch, flags=inside,
    )
    gram = lax.all_to_all(gram.reshape(n_lon, 1, -1), "lon", 0, 0, tiled=True)
    (gram,) = kernel(sum_copies, on_chip((n_lat,) + gram.shape[1:]), gram)
    gram = lax.all_to_all(gram, "lat", 0, 0, tiled=True)
    (gram,) = kernel(sum_copies, on_chip((n_lon,) + gram.shape[1:]), gram)
    gram = lax.all_to_all(gram, "lon", 0, 0, tiled=True)
    cells = 4 * 128 * n_lat * n_lon
    fields, upper = kernel(
        lambda *refs: chol_fields(*refs, cells=cells),
        tuple(jax.ShapeDtypeStruct(s, F32) for s in ((3072, 128), (256, 256))),
        gram.reshape(272, 128), s_low, s_high, scratch=[(256, 512)],
    )
    return (fields.reshape(tangent.shape), upper)


def solution(mesh):
    in_specs = (P(None, None, "lat", "lon"), P(None, "lat", "lon"))
    out_specs = (P(None, None, "lat", "lon"), P())
    return jax.shard_map(
        per_device, mesh=mesh, in_specs=in_specs, out_specs=out_specs, check_vma=False
    )
```

```python
import jax
import jax.numpy as jnp
from jax import lax
from jax.experimental import pallas as pl
from jax.experimental.pallas import tpu as pltpu
from jax.sharding import PartitionSpec as P

HI = lax.Precision.HIGHEST
F32 = jnp.float32


def iota(shape, dim):
    return lax.broadcasted_iota(jnp.int32, shape, dim)


def eight(i, base=0):
    at = base + 8 * i
    return pl.ds(at if isinstance(at, int) else pl.multiple_of(at, 8), 8)


def split_rows(x_hbm, base_hbm, low_ref, high_ref, pack_ref, x_ref, base_ref, sems):
    places = [pl.ds(768 * k, 768) for k in range(4)]
    copies = [pltpu.make_async_copy(x_hbm.at[p], x_ref.at[p], sems.at[k]) for k, p in enumerate(places)]
    base_copy = pltpu.make_async_copy(base_hbm, base_ref, sems.at[4])
    for copy in copies:
        copy.start()
    base_copy.start()
    lane = iota((8, 128), 1)
    slot = lane % 32
    field = lane // 32

    def packed(parts):
        acc = jnp.zeros((8, 128), F32)
        for f, r, part in parts:
            at = 32 * f + 8 * r
            moved = pltpu.roll(part, (at + 2) % 128, 1)
            acc = acc + jnp.where((field == f) & (slot >= 8 * r) & (slot < 8 * r + 4), moved, 0.0)
        return acc + pltpu.roll(acc, 4, 1)

    def chunk(i, carry):
        for half in range(2):
            parts = []
            for f in range(3):
                for r in range(4):
                    part = x_ref[pl.ds(192 * i + 96 * half + 4 * f + r, 8, stride=12), :]
                    ref = low_ref if r < 2 else high_ref
                    start = ((r % 2) * 3 + f) * 256
                    ref[pl.ds(pl.multiple_of(start + 16 * i + 8 * half, 8), 8), :] = part
                    parts.append((f, r, part))
            pack_ref[eight(2 * i + half), :] = packed(parts)
        return carry

    for k, copy in enumerate(copies):
        copy.wait()
        lax.fori_loop(4 * k, 4 * k + 4, chunk, 0, unroll=2)
    base_copy.wait()
    parts = []
    for r in range(4):
        rows = base_ref[pl.ds(r, 4, stride=4), :]
        both = jnp.concatenate([rows, rows], axis=0)
        parts.append((0, r, both))
        if r == 0:
            low_ref[1536:1544, :] = both
        if r == 3:
            high_ref[1536:1544, :] = both
    pack_ref[256:264, :] = packed(parts)


def corners_out(west_ref, east_ref, up_ref, down_ref):
    slot = iota((256, 128), 1) % 8
    joined = jnp.where(slot < 4, west_ref[0:256, :], east_ref[0:256, :])
    row = iota((8, 128), 0)
    lane = iota((8, 128), 1)
    for ref, r in ((up_ref, 3), (down_ref, 0)):
        at = 32 * (row // 2) + 8 * r + jnp.where(row % 2 == 0, 1, 6)
        pick = jnp.where((lane == at) & (row < 6), 1.0, 0.0)
        ref[...] = lax.dot_general(
            pick, joined, (((1,), (1,)), ((), ())), precision=HI, preferred_element_type=F32
        )


def spread_corners(corner, r):
    row = iota((8, 128), 0)
    lane = iota((8, 128), 1)
    at = 32 * (row // 2) + 8 * r
    west = (row % 2 == 0) & (lane == at + 1)
    east = (row % 2 == 1) & ((lane == at) | (lane == at + 6))
    place = jnp.where((west | east) & (row < 6), 1.0, 0.0)
    return lax.dot_general(
        corner, place, (((0,), (0,)), ((), ())), precision=HI, preferred_element_type=F32
    )


def set_coefs(coef_ref, at, lines):
    for plane, line in enumerate(lines):
        coef_ref[4 * at + plane] = jnp.broadcast_to((1.0 if plane == 3 else 0.5) * line, (8, 128))


def edge_lines(pack_ref, west_ref, east_ref):
    slot = iota((1, 128), 1) % 8
    for plane in range(4):
        row = slice(256 + plane, 257 + plane)
        yield jnp.where(slot < 2, west_ref[row, :], jnp.where(slot >= 6, east_ref[row, :], pack_ref[row, :]))


def advanced(coef_ref, at, q, dx, dy):
    a, b, c, d = (coef_ref[4 * at + k] for k in range(4))
    h = q[0] - a * dx[0] - b * dy[0] - c * (dx[1] + dy[2])
    u = q[1] - a * dx[1] - b * dy[1] + d * q[2] - 0.25 * dx[0]
    v = q[2] - a * dx[2] - b * dy[2] - d * q[1] - 0.25 * dy[0]
    return [h, u, v]


def from_north(coef_ref, at, q):
    b, c = (coef_ref[4 * at + k] for k in (1, 2))
    return [-(b * q[0]) - c * q[2], -(b * q[1]), -(b * q[2]) - 0.25 * q[0]]


def minus(q):
    return [-x for x in q]


def plus(p, q):
    return [x + y for x, y in zip(p, q)]


def across(lane, x, ends, r):
    ends = pltpu.roll(ends, (127 - 8 * r) % 128, 1)
    east = jnp.where(lane == 127, ends, pltpu.roll(x, 127, 1))
    west = jnp.where(lane == 0, ends, pltpu.roll(x, 1, 1))
    return east - west


def beside(lane, edge):
    return jnp.where(lane % 8 == 0, pltpu.roll(edge, 122, 1), edge)


def by_field(x):
    return [x, pltpu.roll(x, 96, 1), pltpu.roll(x, 64, 1)]


def read_row(ref, r, i):
    return [ref[eight(i, (3 * r + f) * 256), :] for f in range(3)]


def own_part(
    base_ref, low_ref, high_ref, pack_ref, west_ref, east_ref, s_low_ref, s_high_ref, coef_ref, one_ref, ends_ref
):
    lane = iota((8, 128), 1)
    slot = lane % 8
    for r in range(4):
        set_coefs(coef_ref, r, [base_ref[4 * k + r:4 * k + r + 1, :] for k in range(4)])
    set_coefs(coef_ref, 4, edge_lines(pack_ref, west_ref, east_ref))

    def step(q, ends):
        out = []
        for r in range(4):
            dx = [across(lane, q[r][f], ends[f], r) for f in range(3)]
            if r == 0:
                dy = q[1]
            elif r == 3:
                dy = minus(q[2])
            else:
                dy = plus(q[r + 1], minus(q[r - 1]))
            out.append(advanced(coef_ref, r, q[r], dx, dy))
        return out

    def first(i, carry):
        q = [read_row(low_ref if r < 2 else high_ref, r % 2, i) for r in range(4)]
        at = eight(i)
        joined = jnp.where(slot < 2, west_ref[at, :], jnp.where(slot >= 6, east_ref[at, :], pack_ref[at, :]))
        edge = by_field(joined)
        one = step(q, [beside(lane, e) for e in edge])
        for r in range(4):
            for f in range(3):
                one_ref[3 * r + f, at, :] = one[r][f]
        dx = [pltpu.roll(e, 127, 1) - pltpu.roll(e, 1, 1) for e in edge]
        dy = [
            jnp.where(lane < 24, pltpu.roll(e, 120, 1), 0.0) - jnp.where(lane >= 8, pltpu.roll(e, 8, 1), 0.0)
            for e in edge
        ]
        for f, e in enumerate(advanced(coef_ref, 4, edge, dx, dy)):
            ends_ref[f, at, :] = beside(lane, e)
        return carry

    def second(i, carry):
        at = eight(i)
        one = [[one_ref[3 * r + f, at, :] for f in range(3)] for r in range(4)]
        two = step(one, [ends_ref[f, at, :] for f in range(3)])
        for r in range(4):
            ref = s_low_ref if r < 2 else s_high_ref
            for f in range(3):
                ref[3 * (r % 2) + f, at, :] = two[r][f]
        return carry

    lax.fori_loop(0, 32, first, 0, unroll=2)
    lax.fori_loop(0, 32, second, 0, unroll=8)


def add_side(north, inside, base_ref, half_ref, halo_ref, packs, corner_ref, part_ref, s_ref, coef_ref, spread_ref):
    lane = iota((8, 128), 1)
    sign = (lambda q: q) if north else minus
    near, far = (3, 2) if north else (0, 1)
    spread_ref[...] = spread_corners(corner_ref[...], near)
    set_coefs(coef_ref, 0, [base_ref[4 * k + near:4 * k + near + 1, :] for k in range(4)])
    set_coefs(coef_ref, 1, [base_ref[4 * k + far:4 * k + far + 1, :] for k in range(4)])
    set_coefs(coef_ref, 2, [halo_ref[1536 + k:1537 + k, :] for k in range(4)])
    set_coefs(coef_ref, 3, edge_lines(*packs))

    def chunk(i, carry):
        own = read_row(half_ref, near % 2, i)
        halo = [read_row(halo_ref, k, i) for k in ((0, 1) if north else (1, 0))]
        corner = by_field(spread_ref[eight(i), :])
        dx = [across(lane, halo[0][f], corner[f], near) for f in range(3)]
        dy = sign(plus(halo[1], minus(own)))
        beyond = [x * inside for x in advanced(coef_ref, 2, halo[0], dx, dy)]
        gained = sign(from_north(coef_ref, 0, halo[0]))
        ends = [beside(lane, e) for e in sign(from_north(coef_ref, 3, corner))]
        dx = [across(lane, gained[f], ends[f], near) for f in range(3)]
        first = advanced(coef_ref, 0, gained, dx, sign(beyond))
        second = sign(from_north(coef_ref, 1, gained))
        for f in range(3):
            for r, add in ((near % 2, first), (far % 2, second)):
                s_ref[3 * r + f, eight(i), :] = part_ref[3 * r + f, eight(i), :] + add[f]
        return carry

    if north:
        for i in range(32):
            chunk(i, 0)
    else:
        lax.fori_loop(0, 32, chunk, 0, unroll=4)


def gram_of(s_ref):
    total = jnp.zeros((256, 256), F32)
    for c in range(0, 6, 2):
        both = jnp.concatenate([s_ref[c], s_ref[c + 1]], axis=1)
        total = total + lax.dot_general(
            both, both, (((1,), (1,)), ((), ())), precision=HI, preferred_element_type=F32
        )
    return total


def south_side(
    inside_ref, base_ref, half_ref, halo_ref, pack_ref, west_ref, east_ref, corner_ref, part_ref,
    s_ref, coef_ref, spread_ref,
):
    add_side(False, inside_ref[0].astype(F32), base_ref, half_ref, halo_ref, (pack_ref, west_ref, east_ref),
             corner_ref, part_ref, s_ref, coef_ref, spread_ref)


def north_side(
    inside_ref, base_ref, half_ref, halo_ref, pack_ref, west_ref, east_ref, corner_ref, part_ref, other_ref,
    s_ref, gram_ref, coef_ref, spread_ref,
):
    total = gram_of(other_ref)
    add_side(True, inside_ref[1].astype(F32), base_ref, half_ref, halo_ref, (pack_ref, west_ref, east_ref),
             corner_ref, part_ref, s_ref, coef_ref, spread_ref)
    total = total + gram_of(s_ref)
    row = iota((128, 128), 0)
    col = iota((128, 128), 1)
    corner = total[128:, 128:]
    gram_ref[0:128, :] = jnp.where(row >= col, total[:128, :128], corner)
    gram_ref[128:256, :] = total[128:, :128]
    diagonal = jnp.sum(jnp.where(row == col, corner, 0.0), axis=0, keepdims=True)
    gram_ref[256:272, :] = jnp.where(iota((16, 128), 0) == 0, diagonal, 0.0)


def sum_copies(in_ref, out_ref):
    total = in_ref[0]
    for k in range(1, in_ref.shape[0]):
        total = total + in_ref[k]
    for k in range(out_ref.shape[0]):
        out_ref[k] = total


def lanes_of(x, lane):
    return jnp.broadcast_to(x[:, lane:lane + 1], x.shape)


def row_of(x, row):
    return jnp.broadcast_to(x[row:row + 1, :], x.shape)


def eliminate(m_ref):
    sub = iota((8, 128), 0)
    for panel in range(4):
        j0 = 64 * panel
        td = j0 // 128
        tiles = (0, 1, 2) if td == 0 else (1, 2, 3)
        rows = [{t: m_ref[j0 + 8 * g:j0 + 8 * g + 8, 128 * t:128 * t + 128] for t in tiles} for g in range(8)]
        for b in range(8):
            lane = j0 % 128 + 8 * b
            cols = [[lanes_of(rows[b][td], lane + m) for m in range(8)]]
            work = [dict(rows[g]) for g in range(b, 8)]
            pivot = row_of(cols[0][0], 0)
            steps = []
            for k in range(8):
                r = lax.rsqrt(pivot)
                inv = r * r
                scale = r if k == 0 else jnp.where(sub == k, r, scale)
                line = {m: row_of(cols[0][m], k) for m in range(k + 1, 8)}
                if k < 7:
                    pivot = row_of(cols[0][k + 1], k + 1) - (line[k + 1] * line[k + 1]) * inv
                wide = {t: row_of(work[0][t], k) for t in tiles}
                f = jnp.where(sub > k, cols[0][k] * inv, 0.0)
                for m in range(k + 1, 8):
                    cols[0][m] = cols[0][m] - f * line[m]
                for t in tiles:
                    work[0][t] = work[0][t] - f * wide[t]
                steps.append((inv, line, wide))
            for g in range(1, 8 - b):
                left = [lanes_of(rows[b + g][td], lane + m) for m in range(8)]
                for k, (inv, line, wide) in enumerate(steps):
                    f = left[k] * inv
                    for m in range(k + 1, 8):
                        left[m] = left[m] - f * line[m]
                    for t in tiles:
                        work[g][t] = work[g][t] - f * wide[t]
            for g in range(b, 8):
                rows[g] = work[g - b]
            for t in tiles:
                rows[b][t] = rows[b][t] * scale
                m_ref[j0 + 8 * b:j0 + 8 * b + 8, 128 * t:128 * t + 128] = rows[b][t]
        if panel == 3:
            break
        first = j0 + 64
        top = jnp.concatenate([jnp.concatenate([rows[g][t] for t in tiles], axis=1) for g in range(8)], axis=0)
        spans = []
        for half in range(first // 128, 2):
            begin = max(first, 128 * half)
            end = 128 * half + 128
            if begin == first and True:
                spans.append((half, begin, begin + 64))
                begin += 64
            if begin < end:
                spans.append((half, begin, end))
        turned = {half: top[:, 128 * (half - td):128 * (half - td) + 128].T for half in range(first // 128, 2)}
        for half, begin, end in spans:
            use = top if half == td else top[:, 128:]
            delta = jnp.dot(turned[half][begin - 128 * half:end - 128 * half, :], use, precision=HI, preferred_element_type=F32)
            lo = 128 * tiles[0] if half == td else 128 * tiles[1]
            hi = 128 * (tiles[-1] + 1)
            m_ref[begin:end, lo:hi] = m_ref[begin:end, lo:hi] - delta


def chol_fields(gram_ref, low_ref, high_ref, out_ref, upper_ref, m_ref, *, cells):
    row = iota((128, 128), 0)
    col = iota((128, 128), 1)
    eye = jnp.where(row == col, 1.0, 0.0).astype(F32)
    blank = jnp.zeros((128, 128), F32)
    packed = gram_ref[...] * (1.0 / cells)
    folded = packed[0:128]
    mirrored = folded.T
    m_ref[0:128, 0:128] = jnp.where(row >= col, folded, mirrored)
    m_ref[128:256, 0:128] = packed[128:256]
    m_ref[0:128, 128:256] = packed[128:256].T
    m_ref[128:256, 128:256] = jnp.where(row < col, folded, jnp.where(row > col, mirrored, packed[256:257]))
    m_ref[0:128, 256:384] = eye
    m_ref[0:128, 384:512] = blank
    m_ref[128:256, 256:384] = blank
    m_ref[128:256, 384:512] = eye
    eliminate(m_ref)
    upper_ref[0:128, 0:128] = jnp.where(row <= col, m_ref[0:128, 0:128], 0.0)
    upper_ref[0:128, 128:256] = m_ref[0:128, 128:256]
    upper_ref[128:256, 0:128] = blank
    upper_ref[128:256, 128:256] = jnp.where(row <= col, m_ref[128:256, 128:256], 0.0)
    first = jnp.where(row >= col, m_ref[0:128, 256:384], 0.0)
    second = jnp.concatenate([m_ref[128:256, 256:384], jnp.where(row >= col, m_ref[128:256, 384:512], 0.0)], axis=1)
    inverse = jnp.concatenate([jnp.concatenate([first, blank], axis=1), second], axis=0)
    for half, ref in enumerate((low_ref, high_ref)):
        for c in range(0, 6, 2):
            both = jnp.concatenate([ref[c], ref[c + 1]], axis=1)
            y = jnp.dot(inverse, both, precision=HI, preferred_element_type=F32)
            for k in range(2):
                r, f = divmod(c + k, 3)
                out_ref[pl.ds(4 * f + 2 * half + r, 256, stride=12), :] = y[:, 128 * k:128 * k + 128]


def on_chip(*shapes):
    return tuple(pltpu.VMEM(s, F32) for s in shapes)


def kernel(body, out_shape, *args, scratch=(), flags=None):
    args = [pltpu.with_memory_space_constraint(a, pltpu.VMEM) for a in args]
    specs = [pl.BlockSpec(memory_space=pltpu.VMEM)] * len(args)
    if flags is not None:
        args = [flags] + args
        specs = [pl.BlockSpec(memory_space=pltpu.SMEM)] + specs
    out_specs = tuple(pl.BlockSpec(memory_space=pltpu.VMEM) for _ in out_shape)
    return pl.pallas_call(
        body, out_shape=out_shape, in_specs=specs, out_specs=out_specs,
        scratch_shapes=[pltpu.VMEM(s, F32) for s in scratch],
        compiler_params=pltpu.CompilerParams(vmem_limit_bytes=16 * 2**20),
    )(*args)


def per_device(tangent, base_state):
    n_lat = lax.axis_size("lat")
    n_lon = lax.axis_size("lon")
    x = tangent.reshape(3072, 128)
    base = base_state.reshape(16, 128)
    low, high, pack = pl.pallas_call(
        split_rows, out_shape=on_chip((1544, 128), (1544, 128), (264, 128)),
        in_specs=[pl.BlockSpec(memory_space=pl.ANY)] * 2,
        out_specs=(pl.BlockSpec(memory_space=pltpu.VMEM),) * 3,
        scratch_shapes=[pltpu.VMEM((3072, 128), F32), pltpu.VMEM((16, 128), F32), pltpu.SemaphoreType.DMA((5,))],
        compiler_params=pltpu.CompilerParams(vmem_limit_bytes=16 * 2**20),
    )(*[pltpu.with_memory_space_constraint(a, pltpu.HBM) for a in (x, base)])
    east_ring = [(i, (i + 1) % n_lon) for i in range(n_lon)]
    west_ring = [(j, i) for i, j in east_ring]
    north_line = [(i, i + 1) for i in range(n_lat - 1)]
    south_line = [(j, i) for i, j in north_line]
    south = lax.ppermute(high, "lat", north_line)
    north = lax.ppermute(low, "lat", south_line)
    west = lax.ppermute(pack, "lon", east_ring)
    east = lax.ppermute(pack, "lon", west_ring)
    corner_up, corner_down = kernel(corners_out, on_chip((8, 256), (8, 256)), west, east)
    south_corner = lax.ppermute(corner_up, "lat", north_line)
    north_corner = lax.ppermute(corner_down, "lat", south_line)
    part_low, part_high = kernel(
        own_part, on_chip((6, 256, 128), (6, 256, 128)), base, low, high, pack, west, east, scratch=[(20, 8, 128), (12, 256, 128), (3, 256, 128)]
    )
    index = lax.axis_index("lat")
    inside = jnp.stack([index > 0, index < n_lat - 1]).astype(jnp.int32)
    scratch = [(16, 8, 128), (256, 128)]
    (s_low,) = kernel(
        south_side, on_chip((6, 256, 128)),
        base, low, south, pack, west, east, south_corner, part_low, scratch=scratch, flags=inside,
    )
    s_high, gram = kernel(
        north_side, on_chip((6, 256, 128), (272, 128)),
        base, high, north, pack, west, east, north_corner, part_high, s_low, scratch=scratch, flags=inside,
    )
    gram = lax.all_to_all(gram.reshape(n_lon, 1, -1), "lon", 0, 0, tiled=True)
    (gram,) = kernel(sum_copies, on_chip((n_lat,) + gram.shape[1:]), gram)
    gram = lax.all_to_all(gram, "lat", 0, 0, tiled=True)
    (gram,) = kernel(sum_copies, on_chip((n_lon,) + gram.shape[1:]), gram)
    gram = lax.all_to_all(gram, "lon", 0, 0, tiled=True)
    cells = 4 * 128 * n_lat * n_lon
    fields, upper = kernel(
        lambda *refs: chol_fields(*refs, cells=cells),
        tuple(jax.ShapeDtypeStruct(s, F32) for s in ((3072, 128), (256, 256))),
        gram.reshape(272, 128), s_low, s_high, scratch=[(256, 512)],
    )
    return (fields.reshape(tangent.shape), upper)


def solution(mesh):
    in_specs = (P(None, None, "lat", "lon"), P(None, "lat", "lon"))
    out_specs = (P(None, None, "lat", "lon"), P())
    return jax.shard_map(
        per_device, mesh=mesh, in_specs=in_specs, out_specs=out_specs, check_vma=False
    )
```

```python
import jax
import jax.numpy as jnp
from jax import lax
from jax.experimental import pallas as pl
from jax.experimental.pallas import tpu as pltpu
from jax.sharding import PartitionSpec as P


HI = lax.Precision.HIGHEST
F32 = jnp.float32


def iota(shape, dim):
    return lax.broadcasted_iota(jnp.int32, shape, dim)


def eight(i, base=0):
    at = base + 8 * i
    return pl.ds(at if isinstance(at, int) else pl.multiple_of(at, 8), 8)


def split_rows(x_hbm, base_hbm, low_ref, high_ref, pack_ref, x_ref, base_ref, sems):
    places = [pl.ds(768 * k, 768) for k in range(4)]
    copies = [pltpu.make_async_copy(x_hbm.at[p], x_ref.at[p], sems.at[k]) for k, p in enumerate(places)]
    base_copy = pltpu.make_async_copy(base_hbm, base_ref, sems.at[4])
    for copy in copies:
        copy.start()
    base_copy.start()
    lane = iota((8, 128), 1)
    slot = lane % 32
    field = lane // 32

    def packed(parts):
        acc = jnp.zeros((8, 128), F32)
        for f, r, part in parts:
            at = 32 * f + 8 * r
            moved = pltpu.roll(part, (at + 2) % 128, 1)
            acc = acc + jnp.where((field == f) & (slot >= 8 * r) & (slot < 8 * r + 4), moved, 0.0)
        return acc + pltpu.roll(acc, 4, 1)

    def chunk(i, carry):
        for half in range(2):
            parts = []
            for f in range(3):
                for r in range(4):
                    part = x_ref[pl.ds(192 * i + 96 * half + 4 * f + r, 8, stride=12), :]
                    ref = low_ref if r < 2 else high_ref
                    start = ((r % 2) * 3 + f) * 256
                    ref[pl.ds(pl.multiple_of(start + 16 * i + 8 * half, 8), 8), :] = part
                    parts.append((f, r, part))
            pack_ref[eight(2 * i + half), :] = packed(parts)
        return carry

    for k, copy in enumerate(copies):
        copy.wait()
        lax.fori_loop(4 * k, 4 * k + 4, chunk, 0, unroll=2)
    base_copy.wait()
    parts = []
    for r in range(4):
        rows = base_ref[pl.ds(r, 4, stride=4), :]
        both = jnp.concatenate([rows, rows], axis=0)
        parts.append((0, r, both))
        if r == 0:
            low_ref[1536:1544, :] = both
        if r == 3:
            high_ref[1536:1544, :] = both
    pack_ref[256:264, :] = packed(parts)


def corners_out(west_ref, east_ref, up_ref, down_ref):
    slot = iota((256, 128), 1) % 8
    joined = jnp.where(slot < 4, west_ref[0:256, :], east_ref[0:256, :])
    row = iota((8, 128), 0)
    lane = iota((8, 128), 1)
    for ref, r in ((up_ref, 3), (down_ref, 0)):
        at = 32 * (row // 2) + 8 * r + jnp.where(row % 2 == 0, 1, 6)
        pick = jnp.where((lane == at) & (row < 6), 1.0, 0.0)
        ref[...] = lax.dot_general(
            pick, joined, (((1,), (1,)), ((), ())), precision=HI, preferred_element_type=F32
        )


def spread_corners(corner, r):
    row = iota((8, 128), 0)
    lane = iota((8, 128), 1)
    at = 32 * (row // 2) + 8 * r
    west = (row % 2 == 0) & (lane == at + 1)
    east = (row % 2 == 1) & ((lane == at) | (lane == at + 6))
    place = jnp.where((west | east) & (row < 6), 1.0, 0.0)
    return lax.dot_general(
        corner, place, (((0,), (0,)), ((), ())), precision=HI, preferred_element_type=F32
    )


def set_coefs(coef_ref, at, lines):
    for plane, line in enumerate(lines):
        coef_ref[4 * at + plane] = jnp.broadcast_to((1.0 if plane == 3 else 0.5) * line, (8, 128))


def edge_lines(pack_ref, west_ref, east_ref):
    slot = iota((1, 128), 1) % 8
    for plane in range(4):
        row = slice(256 + plane, 257 + plane)
        yield jnp.where(slot < 2, west_ref[row, :], jnp.where(slot >= 6, east_ref[row, :], pack_ref[row, :]))


def advanced(coef_ref, at, q, dx, dy):
    a, b, c, d = (coef_ref[4 * at + k] for k in range(4))
    h = q[0] - a * dx[0] - b * dy[0] - c * (dx[1] + dy[2])
    u = q[1] - a * dx[1] - b * dy[1] + d * q[2] - 0.25 * dx[0]
    v = q[2] - a * dx[2] - b * dy[2] - d * q[1] - 0.25 * dy[0]
    return [h, u, v]


def from_north(coef_ref, at, q):
    b, c = (coef_ref[4 * at + k] for k in (1, 2))
    return [-(b * q[0]) - c * q[2], -(b * q[1]), -(b * q[2]) - 0.25 * q[0]]


def minus(q):
    return [-x for x in q]


def plus(p, q):
    return [x + y for x, y in zip(p, q)]


def across(lane, x, ends, r):
    ends = pltpu.roll(ends, (127 - 8 * r) % 128, 1)
    east = jnp.where(lane == 127, ends, pltpu.roll(x, 127, 1))
    west = jnp.where(lane == 0, ends, pltpu.roll(x, 1, 1))
    return east - west


def beside(lane, edge):
    return jnp.where(lane % 8 == 0, pltpu.roll(edge, 122, 1), edge)


def by_field(x):
    return [x, pltpu.roll(x, 96, 1), pltpu.roll(x, 64, 1)]


def read_row(ref, r, i):
    return [ref[eight(i, (3 * r + f) * 256), :] for f in range(3)]


def own_part(
    base_ref, low_ref, high_ref, pack_ref, west_ref, east_ref, s_low_ref, s_high_ref, coef_ref, one_ref, ends_ref
):
    lane = iota((8, 128), 1)
    slot = lane % 8
    for r in range(4):
        set_coefs(coef_ref, r, [base_ref[4 * k + r:4 * k + r + 1, :] for k in range(4)])
    set_coefs(coef_ref, 4, edge_lines(pack_ref, west_ref, east_ref))

    def step(q, ends):
        out = []
        for r in range(4):
            dx = [across(lane, q[r][f], ends[f], r) for f in range(3)]
            if r == 0:
                dy = q[1]
            elif r == 3:
                dy = minus(q[2])
            else:
                dy = plus(q[r + 1], minus(q[r - 1]))
            out.append(advanced(coef_ref, r, q[r], dx, dy))
        return out

    def first(i, carry):
        q = [read_row(low_ref if r < 2 else high_ref, r % 2, i) for r in range(4)]
        at = eight(i)
        joined = jnp.where(slot < 2, west_ref[at, :], jnp.where(slot >= 6, east_ref[at, :], pack_ref[at, :]))
        edge = by_field(joined)
        one = step(q, [beside(lane, e) for e in edge])
        for r in range(4):
            for f in range(3):
                one_ref[3 * r + f, at, :] = one[r][f]
        dx = [pltpu.roll(e, 127, 1) - pltpu.roll(e, 1, 1) for e in edge]
        dy = [
            jnp.where(lane < 24, pltpu.roll(e, 120, 1), 0.0) - jnp.where(lane >= 8, pltpu.roll(e, 8, 1), 0.0)
            for e in edge
        ]
        for f, e in enumerate(advanced(coef_ref, 4, edge, dx, dy)):
            ends_ref[f, at, :] = beside(lane, e)
        return carry

    def second(i, carry):
        at = eight(i)
        one = [[one_ref[3 * r + f, at, :] for f in range(3)] for r in range(4)]
        two = step(one, [ends_ref[f, at, :] for f in range(3)])
        for r in range(4):
            ref = s_low_ref if r < 2 else s_high_ref
            for f in range(3):
                ref[3 * (r % 2) + f, at, :] = two[r][f]
        return carry

    lax.fori_loop(0, 32, first, 0, unroll=2)
    lax.fori_loop(0, 32, second, 0, unroll=8)


def add_side(north, inside, base_ref, half_ref, halo_ref, packs, corner_ref, part_ref, s_ref, coef_ref, spread_ref):
    lane = iota((8, 128), 1)
    sign = (lambda q: q) if north else minus
    near, far = (3, 2) if north else (0, 1)
    spread_ref[...] = spread_corners(corner_ref[...], near)
    set_coefs(coef_ref, 0, [base_ref[4 * k + near:4 * k + near + 1, :] for k in range(4)])
    set_coefs(coef_ref, 1, [base_ref[4 * k + far:4 * k + far + 1, :] for k in range(4)])
    set_coefs(coef_ref, 2, [halo_ref[1536 + k:1537 + k, :] for k in range(4)])
    set_coefs(coef_ref, 3, edge_lines(*packs))

    def gained_row(i):
        halo = read_row(halo_ref, 0 if north else 1, i)
        return halo, sign(from_north(coef_ref, 0, halo))

    def add(r, i, extra):
        for f in range(3):
            s_ref[3 * r + f, eight(i), :] = part_ref[3 * r + f, eight(i), :] + extra[f]

    def far_row(i):
        add(far % 2, i, sign(from_north(coef_ref, 1, gained_row(i)[1])))

    def near_row(i):
        own = read_row(half_ref, near % 2, i)
        halo, gained = gained_row(i)
        outer = read_row(halo_ref, 1 if north else 0, i)
        corner = by_field(spread_ref[eight(i), :])
        dx = [across(lane, halo[f], corner[f], near) for f in range(3)]
        dy = sign(plus(outer, minus(own)))
        beyond = [x * inside for x in advanced(coef_ref, 2, halo, dx, dy)]
        ends = [beside(lane, e) for e in sign(from_north(coef_ref, 3, corner))]
        dx = [across(lane, gained[f], ends[f], near) for f in range(3)]
        add(near % 2, i, advanced(coef_ref, 0, gained, dx, sign(beyond)))

    def chunk(i, carry):
        far_row(i)
        near_row(i)
        return carry

    if not north:
        lax.fori_loop(0, 32, chunk, 0, unroll=4)
        return gram_of_row(s_ref, 0) + gram_of_row(s_ref, 1)
    for i in range(32):
        far_row(i)
    total = gram_of_row(s_ref, far % 2)
    for i in range(32):
        near_row(i)
    return total + gram_of_row(s_ref, near % 2)


def gram_of_row(s_ref, r):
    row = jnp.concatenate([s_ref[3 * r + f] for f in range(3)], axis=1)
    return lax.dot_general(row, row, (((1,), (1,)), ((), ())), precision=HI, preferred_element_type=F32)


def south_side(
    inside_ref, base_ref, half_ref, halo_ref, pack_ref, west_ref, east_ref, corner_ref, part_ref,
    s_ref, gram_ref, coef_ref, spread_ref,
):
    gram_ref[...] = add_side(False, inside_ref[0].astype(F32), base_ref, half_ref, halo_ref, (pack_ref, west_ref, east_ref),
             corner_ref, part_ref, s_ref, coef_ref, spread_ref)


def north_side(
    inside_ref, base_ref, half_ref, halo_ref, pack_ref, west_ref, east_ref, corner_ref, part_ref, partial_ref,
    s_ref, gram_ref, coef_ref, spread_ref,
):
    total = add_side(True, inside_ref[1].astype(F32), base_ref, half_ref, halo_ref, (pack_ref, west_ref, east_ref),
             corner_ref, part_ref, s_ref, coef_ref, spread_ref)
    total = total + partial_ref[...]
    row = iota((128, 128), 0)
    col = iota((128, 128), 1)
    corner = total[128:, 128:]
    gram_ref[0:128, :] = jnp.where(row >= col, total[:128, :128], corner)
    gram_ref[128:256, :] = total[128:, :128]
    diagonal = jnp.sum(jnp.where(row == col, corner, 0.0), axis=0, keepdims=True)
    gram_ref[256:272, :] = jnp.where(iota((16, 128), 0) == 0, diagonal, 0.0)


def sum_copies(in_ref, out_ref):
    total = in_ref[0]
    for k in range(1, in_ref.shape[0]):
        total = total + in_ref[k]
    for k in range(out_ref.shape[0]):
        out_ref[k] = total


def lanes_of(x, lane):
    return jnp.broadcast_to(x[:, lane:lane + 1], x.shape)


def row_of(x, row):
    return jnp.broadcast_to(x[row:row + 1, :], x.shape)


def eliminate(m_ref):
    sub = iota((8, 128), 0)
    for panel in range(4):
        j0 = 64 * panel
        td = j0 // 128
        tiles = (0, 1, 2) if td == 0 else (1, 2, 3)
        rows = [{t: m_ref[j0 + 8 * g:j0 + 8 * g + 8, 128 * t:128 * t + 128] for t in tiles} for g in range(8)]
        for b in range(8):
            lane = j0 % 128 + 8 * b
            cols = [[lanes_of(rows[b][td], lane + m) for m in range(8)]]
            work = [dict(rows[g]) for g in range(b, 8)]
            pivot = row_of(cols[0][0], 0)
            steps = []
            for k in range(8):
                r = lax.rsqrt(pivot)
                inv = r * r
                scale = r if k == 0 else jnp.where(sub == k, r, scale)
                line = {m: row_of(cols[0][m], k) for m in range(k + 1, 8)}
                if k < 7:
                    pivot = row_of(cols[0][k + 1], k + 1) - (line[k + 1] * line[k + 1]) * inv
                wide = {t: row_of(work[0][t], k) for t in tiles}
                f = jnp.where(sub > k, cols[0][k] * inv, 0.0)
                for m in range(k + 1, 8):
                    cols[0][m] = cols[0][m] - f * line[m]
                for t in tiles:
                    work[0][t] = work[0][t] - f * wide[t]
                steps.append((inv, line, wide))
            for g in range(1, 8 - b):
                left = [lanes_of(rows[b + g][td], lane + m) for m in range(8)]
                for k, (inv, line, wide) in enumerate(steps):
                    f = left[k] * inv
                    for m in range(k + 1, 8):
                        left[m] = left[m] - f * line[m]
                    for t in tiles:
                        work[g][t] = work[g][t] - f * wide[t]
            for g in range(b, 8):
                rows[g] = work[g - b]
            for t in tiles:
                rows[b][t] = rows[b][t] * scale
                m_ref[j0 + 8 * b:j0 + 8 * b + 8, 128 * t:128 * t + 128] = rows[b][t]
        if panel == 3:
            break
        first = j0 + 64
        top = jnp.concatenate([jnp.concatenate([rows[g][t] for t in tiles], axis=1) for g in range(8)], axis=0)
        spans = []
        for half in range(first // 128, 2):
            begin = max(first, 128 * half)
            end = 128 * half + 128
            if begin == first and True:
                spans.append((half, begin, begin + 64))
                begin += 64
            if begin < end:
                spans.append((half, begin, end))
        turned = {half: top[:, 128 * (half - td):128 * (half - td) + 128].T for half in range(first // 128, 2)}
        for half, begin, end in spans:
            use = top if half == td else top[:, 128:]
            delta = jnp.dot(turned[half][begin - 128 * half:end - 128 * half, :], use, precision=HI, preferred_element_type=F32)
            lo = 128 * tiles[0] if half == td else 128 * tiles[1]
            hi = 128 * (tiles[-1] + 1)
            m_ref[begin:end, lo:hi] = m_ref[begin:end, lo:hi] - delta


def chol_fields(gram_ref, low_ref, high_ref, out_ref, upper_ref, m_ref, *, cells):
    row = iota((128, 128), 0)
    col = iota((128, 128), 1)
    eye = jnp.where(row == col, 1.0, 0.0).astype(F32)
    blank = jnp.zeros((128, 128), F32)
    packed = gram_ref[...] * (1.0 / cells)
    folded = packed[0:128]
    mirrored = folded.T
    m_ref[0:128, 0:128] = jnp.where(row >= col, folded, mirrored)
    m_ref[128:256, 0:128] = packed[128:256]
    m_ref[0:128, 128:256] = packed[128:256].T
    m_ref[128:256, 128:256] = jnp.where(row < col, folded, jnp.where(row > col, mirrored, packed[256:257]))
    m_ref[0:128, 256:384] = eye
    m_ref[0:128, 384:512] = blank
    m_ref[128:256, 256:384] = blank
    m_ref[128:256, 384:512] = eye
    eliminate(m_ref)
    upper_ref[0:128, 0:128] = jnp.where(row <= col, m_ref[0:128, 0:128], 0.0)
    upper_ref[0:128, 128:256] = m_ref[0:128, 128:256]
    upper_ref[128:256, 0:128] = blank
    upper_ref[128:256, 128:256] = jnp.where(row <= col, m_ref[128:256, 128:256], 0.0)
    first = jnp.where(row >= col, m_ref[0:128, 256:384], 0.0)
    second = jnp.concatenate([m_ref[128:256, 256:384], jnp.where(row >= col, m_ref[128:256, 384:512], 0.0)], axis=1)
    inverse = jnp.concatenate([jnp.concatenate([first, blank], axis=1), second], axis=0)
    for half, ref in enumerate((low_ref, high_ref)):
        for c in range(0, 6, 2):
            both = jnp.concatenate([ref[c], ref[c + 1]], axis=1)
            y = jnp.dot(inverse, both, precision=HI, preferred_element_type=F32)
            for k in range(2):
                r, f = divmod(c + k, 3)
                out_ref[pl.ds(4 * f + 2 * half + r, 256, stride=12), :] = y[:, 128 * k:128 * k + 128]


def on_chip(*shapes):
    return tuple(pltpu.VMEM(s, F32) for s in shapes)


def kernel(body, out_shape, *args, scratch=(), flags=None):
    args = [pltpu.with_memory_space_constraint(a, pltpu.VMEM) for a in args]
    specs = [pl.BlockSpec(memory_space=pltpu.VMEM)] * len(args)
    if flags is not None:
        args = [flags] + args
        specs = [pl.BlockSpec(memory_space=pltpu.SMEM)] + specs
    out_specs = tuple(pl.BlockSpec(memory_space=pltpu.VMEM) for _ in out_shape)
    return pl.pallas_call(
        body, out_shape=out_shape, in_specs=specs, out_specs=out_specs,
        scratch_shapes=[pltpu.VMEM(s, F32) for s in scratch],
        compiler_params=pltpu.CompilerParams(vmem_limit_bytes=16 * 2**20),
    )(*args)


def per_device(tangent, base_state):
    n_lat = lax.axis_size("lat")
    n_lon = lax.axis_size("lon")
    x = tangent.reshape(3072, 128)
    base = base_state.reshape(16, 128)
    low, high, pack = pl.pallas_call(
        split_rows, out_shape=on_chip((1544, 128), (1544, 128), (264, 128)),
        in_specs=[pl.BlockSpec(memory_space=pl.ANY)] * 2,
        out_specs=(pl.BlockSpec(memory_space=pltpu.VMEM),) * 3,
        scratch_shapes=[pltpu.VMEM((3072, 128), F32), pltpu.VMEM((16, 128), F32), pltpu.SemaphoreType.DMA((5,))],
        compiler_params=pltpu.CompilerParams(vmem_limit_bytes=16 * 2**20),
    )(*[pltpu.with_memory_space_constraint(a, pltpu.HBM) for a in (x, base)])
    east_ring = [(i, (i + 1) % n_lon) for i in range(n_lon)]
    west_ring = [(j, i) for i, j in east_ring]
    north_line = [(i, i + 1) for i in range(n_lat - 1)]
    south_line = [(j, i) for i, j in north_line]
    south = lax.ppermute(high, "lat", north_line)
    west = lax.ppermute(pack, "lon", east_ring)
    east = lax.ppermute(pack, "lon", west_ring)
    north = lax.ppermute(low, "lat", south_line)
    corner_up, corner_down = kernel(corners_out, on_chip((8, 256), (8, 256)), west, east)
    south_corner = lax.ppermute(corner_up, "lat", north_line)
    north_corner = lax.ppermute(corner_down, "lat", south_line)
    part_low, part_high = kernel(
        own_part, on_chip((6, 256, 128), (6, 256, 128)), base, low, high, pack, west, east, scratch=[(20, 8, 128), (12, 256, 128), (3, 256, 128)]
    )
    index = lax.axis_index("lat")
    inside = jnp.stack([index > 0, index < n_lat - 1]).astype(jnp.int32)
    scratch = [(16, 8, 128), (256, 128)]
    s_low, gram = kernel(
        south_side, on_chip((6, 256, 128), (256, 256)),
        base, low, south, pack, west, east, south_corner, part_low, scratch=scratch, flags=inside,
    )
    s_high, gram = kernel(
        north_side, on_chip((6, 256, 128), (272, 128)),
        base, high, north, pack, west, east, north_corner, part_high, gram, scratch=scratch, flags=inside,
    )
    gram = lax.all_to_all(gram.reshape(n_lon, 1, -1), "lon", 0, 0, tiled=True)
    (gram,) = kernel(sum_copies, on_chip((n_lat,) + gram.shape[1:]), gram)
    gram = lax.all_to_all(gram, "lat", 0, 0, tiled=True)
    (gram,) = kernel(sum_copies, on_chip((n_lon,) + gram.shape[1:]), gram)
    gram = lax.all_to_all(gram, "lon", 0, 0, tiled=True)
    cells = 4 * 128 * n_lat * n_lon
    fields, upper = kernel(
        lambda *refs: chol_fields(*refs, cells=cells),
        tuple(jax.ShapeDtypeStruct(s, F32) for s in ((3072, 128), (256, 256))),
        gram.reshape(272, 128), s_low, s_high, scratch=[(256, 512)],
    )
    return (fields.reshape(tangent.shape), upper)


def solution(mesh):
    in_specs = (P(None, None, "lat", "lon"), P(None, "lat", "lon"))
    out_specs = (P(None, None, "lat", "lon"), P())
    return jax.shard_map(
        per_device, mesh=mesh, in_specs=in_specs, out_specs=out_specs, check_vma=False
    )
```

```python
import jax
import jax.numpy as jnp
from jax import lax
from jax.experimental import pallas as pl
from jax.experimental.pallas import tpu as pltpu
from jax.sharding import PartitionSpec as P


HI = lax.Precision.HIGHEST
F32 = jnp.float32


def iota(shape, dim):
    return lax.broadcasted_iota(jnp.int32, shape, dim)


def eight(i, base=0):
    at = base + 8 * i
    return pl.ds(at if isinstance(at, int) else pl.multiple_of(at, 8), 8)


def split_rows(x_hbm, base_hbm, low_ref, high_ref, pack_ref, x_ref, base_ref, sems):
    places = [pl.ds(768 * k, 768) for k in range(4)]
    copies = [pltpu.make_async_copy(x_hbm.at[p], x_ref.at[p], sems.at[k]) for k, p in enumerate(places)]
    base_copy = pltpu.make_async_copy(base_hbm, base_ref, sems.at[4])
    for copy in copies:
        copy.start()
    base_copy.start()
    lane = iota((8, 128), 1)
    slot = lane % 32
    field = lane // 32

    def packed(parts):
        acc = jnp.zeros((8, 128), F32)
        for f, r, part in parts:
            at = 32 * f + 8 * r
            moved = pltpu.roll(part, (at + 2) % 128, 1)
            acc = acc + jnp.where((field == f) & (slot >= 8 * r) & (slot < 8 * r + 4), moved, 0.0)
        return acc + pltpu.roll(acc, 4, 1)

    def chunk(i, carry):
        for half in range(2):
            parts = []
            for f in range(3):
                for r in range(4):
                    part = x_ref[pl.ds(192 * i + 96 * half + 4 * f + r, 8, stride=12), :]
                    ref = low_ref if r < 2 else high_ref
                    start = ((r % 2) * 3 + f) * 256
                    ref[pl.ds(pl.multiple_of(start + 16 * i + 8 * half, 8), 8), :] = part
                    parts.append((f, r, part))
            pack_ref[eight(2 * i + half), :] = packed(parts)
        return carry

    for k, copy in enumerate(copies):
        copy.wait()
        lax.fori_loop(4 * k, 4 * k + 4, chunk, 0, unroll=2)
    base_copy.wait()
    parts = []
    for r in range(4):
        rows = base_ref[pl.ds(r, 4, stride=4), :]
        both = jnp.concatenate([rows, rows], axis=0)
        parts.append((0, r, both))
        if r == 0:
            low_ref[1536:1544, :] = both
        if r == 3:
            high_ref[1536:1544, :] = both
    pack_ref[256:264, :] = packed(parts)


def corners_out(west_ref, east_ref, up_ref, down_ref):
    slot = iota((256, 128), 1) % 8
    joined = jnp.where(slot < 4, west_ref[0:256, :], east_ref[0:256, :])
    row = iota((8, 128), 0)
    lane = iota((8, 128), 1)
    for ref, r in ((up_ref, 3), (down_ref, 0)):
        at = 32 * (row // 2) + 8 * r + jnp.where(row % 2 == 0, 1, 6)
        pick = jnp.where((lane == at) & (row < 6), 1.0, 0.0)
        ref[...] = lax.dot_general(
            pick, joined, (((1,), (1,)), ((), ())), precision=HI, preferred_element_type=F32
        )


def spread_corners(corner, r):
    row = iota((8, 128), 0)
    lane = iota((8, 128), 1)
    at = 32 * (row // 2) + 8 * r
    west = (row % 2 == 0) & (lane == at + 1)
    east = (row % 2 == 1) & ((lane == at) | (lane == at + 6))
    place = jnp.where((west | east) & (row < 6), 1.0, 0.0)
    return lax.dot_general(
        corner, place, (((0,), (0,)), ((), ())), precision=HI, preferred_element_type=F32
    )


def set_coefs(coef_ref, at, lines):
    for plane, line in enumerate(lines):
        coef_ref[4 * at + plane] = jnp.broadcast_to((1.0 if plane == 3 else 0.5) * line, (8, 128))


def edge_lines(pack_ref, west_ref, east_ref):
    slot = iota((1, 128), 1) % 8
    for plane in range(4):
        row = slice(256 + plane, 257 + plane)
        yield jnp.where(slot < 2, west_ref[row, :], jnp.where(slot >= 6, east_ref[row, :], pack_ref[row, :]))


def advanced(coef_ref, at, q, dx, dy):
    a, b, c, d = (coef_ref[4 * at + k] for k in range(4))
    h = q[0] - a * dx[0] - b * dy[0] - c * (dx[1] + dy[2])
    u = q[1] - a * dx[1] - b * dy[1] + d * q[2] - 0.25 * dx[0]
    v = q[2] - a * dx[2] - b * dy[2] - d * q[1] - 0.25 * dy[0]
    return [h, u, v]


def from_north(coef_ref, at, q):
    b, c = (coef_ref[4 * at + k] for k in (1, 2))
    return [-(b * q[0]) - c * q[2], -(b * q[1]), -(b * q[2]) - 0.25 * q[0]]


def minus(q):
    return [-x for x in q]


def plus(p, q):
    return [x + y for x, y in zip(p, q)]


def across(lane, x, ends, r):
    ends = pltpu.roll(ends, (127 - 8 * r) % 128, 1)
    east = jnp.where(lane == 127, ends, pltpu.roll(x, 127, 1))
    west = jnp.where(lane == 0, ends, pltpu.roll(x, 1, 1))
    return east - west


def beside(lane, edge):
    return jnp.where(lane % 8 == 0, pltpu.roll(edge, 122, 1), edge)


def by_field(x):
    return [x, pltpu.roll(x, 96, 1), pltpu.roll(x, 64, 1)]


def read_row(ref, r, i):
    return [ref[eight(i, (3 * r + f) * 256), :] for f in range(3)]


def own_part(
    base_ref, low_ref, high_ref, pack_ref, west_ref, east_ref, s_low_ref, s_high_ref, coef_ref, one_ref, ends_ref
):
    lane = iota((8, 128), 1)
    slot = lane % 8
    for r in range(4):
        set_coefs(coef_ref, r, [base_ref[4 * k + r:4 * k + r + 1, :] for k in range(4)])
    set_coefs(coef_ref, 4, edge_lines(pack_ref, west_ref, east_ref))

    def step(q, ends):
        out = []
        for r in range(4):
            dx = [across(lane, q[r][f], ends[f], r) for f in range(3)]
            if r == 0:
                dy = q[1]
            elif r == 3:
                dy = minus(q[2])
            else:
                dy = plus(q[r + 1], minus(q[r - 1]))
            out.append(advanced(coef_ref, r, q[r], dx, dy))
        return out

    def first(i, carry):
        q = [read_row(low_ref if r < 2 else high_ref, r % 2, i) for r in range(4)]
        at = eight(i)
        joined = jnp.where(slot < 2, west_ref[at, :], jnp.where(slot >= 6, east_ref[at, :], pack_ref[at, :]))
        edge = by_field(joined)
        one = step(q, [beside(lane, e) for e in edge])
        for r in range(4):
            for f in range(3):
                one_ref[3 * r + f, at, :] = one[r][f]
        dx = [pltpu.roll(e, 127, 1) - pltpu.roll(e, 1, 1) for e in edge]
        dy = [
            jnp.where(lane < 24, pltpu.roll(e, 120, 1), 0.0) - jnp.where(lane >= 8, pltpu.roll(e, 8, 1), 0.0)
            for e in edge
        ]
        for f, e in enumerate(advanced(coef_ref, 4, edge, dx, dy)):
            ends_ref[f, at, :] = beside(lane, e)
        return carry

    def second(i, carry):
        at = eight(i)
        one = [[one_ref[3 * r + f, at, :] for f in range(3)] for r in range(4)]
        two = step(one, [ends_ref[f, at, :] for f in range(3)])
        for r in range(4):
            ref = s_low_ref if r < 2 else s_high_ref
            for f in range(3):
                ref[3 * (r % 2) + f, at, :] = two[r][f]
        return carry

    lax.fori_loop(0, 32, first, 0, unroll=2)
    lax.fori_loop(0, 32, second, 0, unroll=8)


def add_side(north, inside, base_ref, half_ref, halo_ref, packs, corner_ref, part_ref, s_ref, coef_ref, spread_ref):
    lane = iota((8, 128), 1)
    sign = (lambda q: q) if north else minus
    near, far = (3, 2) if north else (0, 1)
    spread_ref[...] = spread_corners(corner_ref[...], near)
    set_coefs(coef_ref, 0, [base_ref[4 * k + near:4 * k + near + 1, :] for k in range(4)])
    set_coefs(coef_ref, 1, [base_ref[4 * k + far:4 * k + far + 1, :] for k in range(4)])
    set_coefs(coef_ref, 2, [halo_ref[1536 + k:1537 + k, :] for k in range(4)])
    set_coefs(coef_ref, 3, edge_lines(*packs))

    def gained_row(i):
        halo = read_row(halo_ref, 0 if north else 1, i)
        return halo, sign(from_north(coef_ref, 0, halo))

    def add(r, i, extra):
        for f in range(3):
            s_ref[3 * r + f, eight(i), :] = part_ref[3 * r + f, eight(i), :] + extra[f]

    def far_row(i):
        add(far % 2, i, sign(from_north(coef_ref, 1, gained_row(i)[1])))

    def near_row(i):
        own = read_row(half_ref, near % 2, i)
        halo, gained = gained_row(i)
        outer = read_row(halo_ref, 1 if north else 0, i)
        corner = by_field(spread_ref[eight(i), :])
        dx = [across(lane, halo[f], corner[f], near) for f in range(3)]
        dy = sign(plus(outer, minus(own)))
        beyond = [x * inside for x in advanced(coef_ref, 2, halo, dx, dy)]
        ends = [beside(lane, e) for e in sign(from_north(coef_ref, 3, corner))]
        dx = [across(lane, gained[f], ends[f], near) for f in range(3)]
        add(near % 2, i, advanced(coef_ref, 0, gained, dx, sign(beyond)))

    def chunk(i, carry):
        far_row(i)
        near_row(i)
        return carry

    if not north:
        lax.fori_loop(0, 32, chunk, 0, unroll=4)
        return gram_of_row(s_ref, 0) + gram_of_row(s_ref, 1)
    for i in range(32):
        far_row(i)
    total = gram_of_row(s_ref, far % 2)
    for i in range(32):
        near_row(i)
    return total + gram_of_row(s_ref, near % 2)


def gram_of_row(s_ref, r):
    row = jnp.concatenate([s_ref[3 * r + f] for f in range(3)], axis=1)
    return lax.dot_general(row, row, (((1,), (1,)), ((), ())), precision=HI, preferred_element_type=F32)


def south_side(
    inside_ref, base_ref, half_ref, halo_ref, pack_ref, west_ref, east_ref, corner_ref, part_ref,
    s_ref, gram_ref, coef_ref, spread_ref,
):
    gram_ref[...] = add_side(False, inside_ref[0].astype(F32), base_ref, half_ref, halo_ref, (pack_ref, west_ref, east_ref),
             corner_ref, part_ref, s_ref, coef_ref, spread_ref)


def north_side(
    inside_ref, base_ref, half_ref, halo_ref, pack_ref, west_ref, east_ref, corner_ref, part_ref, partial_ref,
    s_ref, gram_ref, coef_ref, spread_ref,
):
    total = add_side(True, inside_ref[1].astype(F32), base_ref, half_ref, halo_ref, (pack_ref, west_ref, east_ref),
             corner_ref, part_ref, s_ref, coef_ref, spread_ref)
    total = total + partial_ref[...]
    row = iota((128, 128), 0)
    col = iota((128, 128), 1)
    corner = total[128:, 128:]
    gram_ref[0:128, :] = jnp.where(row >= col, total[:128, :128], corner)
    gram_ref[128:256, :] = total[128:, :128]
    diagonal = jnp.sum(jnp.where(row == col, corner, 0.0), axis=0, keepdims=True)
    gram_ref[256:272, :] = jnp.where(iota((16, 128), 0) == 0, diagonal, 0.0)


def sum_copies(in_ref, out_ref):
    total = in_ref[0]
    for k in range(1, in_ref.shape[0]):
        total = total + in_ref[k]
    for k in range(out_ref.shape[0]):
        out_ref[k] = total


def lanes_of(x, lane):
    return jnp.broadcast_to(x[:, lane:lane + 1], x.shape)


def row_of(x, row):
    return jnp.broadcast_to(x[row:row + 1, :], x.shape)


def eliminate(m_ref):
    sub = iota((8, 128), 0)
    for panel in range(4):
        j0 = 64 * panel
        td = j0 // 128
        tiles = (0, 1, 2) if td == 0 else (1, 2, 3)
        rows = [{t: m_ref[j0 + 8 * g:j0 + 8 * g + 8, 128 * t:128 * t + 128] for t in tiles} for g in range(8)]
        for b in range(8):
            lane = j0 % 128 + 8 * b
            cols = [[lanes_of(rows[b][td], lane + m) for m in range(8)]]
            work = [dict(rows[g]) for g in range(b, 8)]
            pivot = row_of(cols[0][0], 0)
            steps = []
            for k in range(8):
                r = lax.rsqrt(pivot)
                inv = r * r
                scale = r if k == 0 else jnp.where(sub == k, r, scale)
                line = {m: row_of(cols[0][m], k) for m in range(k + 1, 8)}
                if k < 7:
                    pivot = row_of(cols[0][k + 1], k + 1) - (line[k + 1] * line[k + 1]) * inv
                wide = {t: row_of(work[0][t], k) for t in tiles}
                f = jnp.where(sub > k, cols[0][k] * inv, 0.0)
                for m in range(k + 1, 8):
                    cols[0][m] = cols[0][m] - f * line[m]
                for t in tiles:
                    work[0][t] = work[0][t] - f * wide[t]
                steps.append((inv, line, wide))
            for g in range(1, 8 - b):
                left = [lanes_of(rows[b + g][td], lane + m) for m in range(8)]
                for k, (inv, line, wide) in enumerate(steps):
                    f = left[k] * inv
                    for m in range(k + 1, 8):
                        left[m] = left[m] - f * line[m]
                    for t in tiles:
                        work[g][t] = work[g][t] - f * wide[t]
            for g in range(b, 8):
                rows[g] = work[g - b]
            for t in tiles:
                rows[b][t] = rows[b][t] * scale
                m_ref[j0 + 8 * b:j0 + 8 * b + 8, 128 * t:128 * t + 128] = rows[b][t]
        if panel == 3:
            break
        first = j0 + 64
        top = jnp.concatenate([jnp.concatenate([rows[g][t] for t in tiles], axis=1) for g in range(8)], axis=0)
        spans = []
        for half in range(first // 128, 2):
            begin = max(first, 128 * half)
            end = 128 * half + 128
            if begin == first and True:
                spans.append((half, begin, begin + 64))
                begin += 64
            if begin < end:
                spans.append((half, begin, end))
        turned = {half: top[:, 128 * (half - td):128 * (half - td) + 128].T for half in range(first // 128, 2)}
        for half, begin, end in spans:
            use = top if half == td else top[:, 128:]
            delta = jnp.dot(turned[half][begin - 128 * half:end - 128 * half, :], use, precision=HI, preferred_element_type=F32)
            lo = 128 * tiles[0] if half == td else 128 * tiles[1]
            hi = 128 * (tiles[-1] + 1)
            m_ref[begin:end, lo:hi] = m_ref[begin:end, lo:hi] - delta


def chol_fields(gram_ref, low_ref, high_ref, out_hbm, upper_ref, m_ref, out_ref, sems, *, cells):
    row = iota((128, 128), 0)
    col = iota((128, 128), 1)
    eye = jnp.where(row == col, 1.0, 0.0).astype(F32)
    blank = jnp.zeros((128, 128), F32)
    packed = gram_ref[...] * (1.0 / cells)
    folded = packed[0:128]
    mirrored = folded.T
    m_ref[0:128, 0:128] = jnp.where(row >= col, folded, mirrored)
    m_ref[128:256, 0:128] = packed[128:256]
    m_ref[0:128, 128:256] = packed[128:256].T
    m_ref[128:256, 128:256] = jnp.where(row < col, folded, jnp.where(row > col, mirrored, packed[256:257]))
    m_ref[0:128, 256:384] = eye
    m_ref[0:128, 384:512] = blank
    m_ref[128:256, 256:384] = blank
    m_ref[128:256, 384:512] = eye
    eliminate(m_ref)
    first = jnp.where(row >= col, m_ref[0:128, 256:384], 0.0)
    second = jnp.concatenate([m_ref[128:256, 256:384], jnp.where(row >= col, m_ref[128:256, 384:512], 0.0)], axis=1)
    copies = []
    for k, inverse in enumerate((first, second)):
        for half, ref in enumerate((low_ref, high_ref)):
            for c in range(0, 6, 2):
                both = jnp.concatenate([ref[c, 0:128 * k + 128, :], ref[c + 1, 0:128 * k + 128, :]], axis=1)
                y = jnp.dot(inverse, both, precision=HI, preferred_element_type=F32)
                for j in range(2):
                    r, f = divmod(c + j, 3)
                    place = pl.ds(1536 * k + 4 * f + 2 * half + r, 128, stride=12)
                    out_ref[place, :] = y[:, 128 * j:128 * j + 128]
        place = pl.ds(1536 * k, 1536)
        copies.append(pltpu.make_async_copy(out_ref.at[place], out_hbm.at[place], sems.at[k]))
        copies[k].start()
    upper_ref[0:128, 0:128] = jnp.where(row <= col, m_ref[0:128, 0:128], 0.0)
    upper_ref[0:128, 128:256] = m_ref[0:128, 128:256]
    upper_ref[128:256, 0:128] = blank
    upper_ref[128:256, 128:256] = jnp.where(row <= col, m_ref[128:256, 128:256], 0.0)
    for copy in copies:
        copy.wait()


def on_chip(*shapes):
    return tuple(pltpu.VMEM(s, F32) for s in shapes)


def kernel(body, out_shape, *args, scratch=(), flags=None):
    args = [pltpu.with_memory_space_constraint(a, pltpu.VMEM) for a in args]
    specs = [pl.BlockSpec(memory_space=pltpu.VMEM)] * len(args)
    if flags is not None:
        args = [flags] + args
        specs = [pl.BlockSpec(memory_space=pltpu.SMEM)] + specs
    out_specs = tuple(pl.BlockSpec(memory_space=pltpu.VMEM) for _ in out_shape)
    return pl.pallas_call(
        body, out_shape=out_shape, in_specs=specs, out_specs=out_specs,
        scratch_shapes=[pltpu.VMEM(s, F32) for s in scratch],
        compiler_params=pltpu.CompilerParams(vmem_limit_bytes=16 * 2**20),
    )(*args)


def per_device(tangent, base_state):
    n_lat = lax.axis_size("lat")
    n_lon = lax.axis_size("lon")
    x = tangent.reshape(3072, 128)
    base = base_state.reshape(16, 128)
    low, high, pack = pl.pallas_call(
        split_rows, out_shape=on_chip((1544, 128), (1544, 128), (264, 128)),
        in_specs=[pl.BlockSpec(memory_space=pl.ANY)] * 2,
        out_specs=(pl.BlockSpec(memory_space=pltpu.VMEM),) * 3,
        scratch_shapes=[pltpu.VMEM((3072, 128), F32), pltpu.VMEM((16, 128), F32), pltpu.SemaphoreType.DMA((5,))],
        compiler_params=pltpu.CompilerParams(vmem_limit_bytes=16 * 2**20),
    )(*[pltpu.with_memory_space_constraint(a, pltpu.HBM) for a in (x, base)])
    east_ring = [(i, (i + 1) % n_lon) for i in range(n_lon)]
    west_ring = [(j, i) for i, j in east_ring]
    north_line = [(i, i + 1) for i in range(n_lat - 1)]
    south_line = [(j, i) for i, j in north_line]
    south = lax.ppermute(high, "lat", north_line)
    west = lax.ppermute(pack, "lon", east_ring)
    east = lax.ppermute(pack, "lon", west_ring)
    north = lax.ppermute(low, "lat", south_line)
    corner_up, corner_down = kernel(corners_out, on_chip((8, 256), (8, 256)), west, east)
    south_corner = lax.ppermute(corner_up, "lat", north_line)
    north_corner = lax.ppermute(corner_down, "lat", south_line)
    part_low, part_high = kernel(
        own_part, on_chip((6, 256, 128), (6, 256, 128)), base, low, high, pack, west, east, scratch=[(20, 8, 128), (12, 256, 128), (3, 256, 128)]
    )
    index = lax.axis_index("lat")
    inside = jnp.stack([index > 0, index < n_lat - 1]).astype(jnp.int32)
    scratch = [(16, 8, 128), (256, 128)]
    s_low, gram = kernel(
        south_side, on_chip((6, 256, 128), (256, 256)),
        base, low, south, pack, west, east, south_corner, part_low, scratch=scratch, flags=inside,
    )
    s_high, gram = kernel(
        north_side, on_chip((6, 256, 128), (272, 128)),
        base, high, north, pack, west, east, north_corner, part_high, gram, scratch=scratch, flags=inside,
    )
    gram = lax.all_to_all(gram.reshape(n_lon, 1, -1), "lon", 0, 0, tiled=True)
    (gram,) = kernel(sum_copies, on_chip((n_lat,) + gram.shape[1:]), gram)
    gram = lax.all_to_all(gram, "lat", 0, 0, tiled=True)
    (gram,) = kernel(sum_copies, on_chip((n_lon,) + gram.shape[1:]), gram)
    gram = lax.all_to_all(gram, "lon", 0, 0, tiled=True)
    cells = 4 * 128 * n_lat * n_lon
    args = [pltpu.with_memory_space_constraint(a, pltpu.VMEM) for a in (gram.reshape(272, 128), s_low, s_high)]
    vmem = pl.BlockSpec(memory_space=pltpu.VMEM)
    fields, upper = pl.pallas_call(
        lambda *refs: chol_fields(*refs, cells=cells),
        out_shape=tuple(jax.ShapeDtypeStruct(s, F32) for s in ((3072, 128), (256, 256))),
        in_specs=[vmem] * 3, out_specs=(pl.BlockSpec(memory_space=pl.ANY), vmem),
        scratch_shapes=[pltpu.VMEM((256, 512), F32), pltpu.VMEM((3072, 128), F32), pltpu.SemaphoreType.DMA((2,))],
        compiler_params=pltpu.CompilerParams(vmem_limit_bytes=16 * 2**20),
    )(*args)
    return (fields.reshape(tangent.shape), upper)


def solution(mesh):
    in_specs = (P(None, None, "lat", "lon"), P(None, "lat", "lon"))
    out_specs = (P(None, None, "lat", "lon"), P())
    return jax.shard_map(
        per_device, mesh=mesh, in_specs=in_specs, out_specs=out_specs, check_vma=False
    )
```
